32 devices in a mesh: layer: 8 (over z, y), latent: 4 (over x, core).
Axes of the slice: x: 2, y: 2, z: 4, core: 2. Of those that a mesh axis runs over, the one named last changes fastest.
Arguments:
- layer_inputs: bfloat16 [384, 8192], P('latent', 'layer'), may hold values from -6 to 6
- mlp_outputs: bfloat16 [384, 8192], P('latent', 'layer'), may hold values from -6 to 6
- enc_weight: bfloat16 [8192, 4096], P('layer', 'latent'), may hold values from -0.125 to 0.125
- enc_bias: float32 [4, 4096], P(None, 'latent'), may hold values from -1 to 0.5
- dec_weight: bfloat16 [4, 4096, 8192], P(None, 'latent', 'layer'), may hold values from -0.046875 to 0.046875
Outputs:
- enc_grad: float32 [8192, 4096], P('layer', 'latent')
- dec_grad: bfloat16 [4, 4096, 8192], P(None, 'latent', 'layer')
The draws below stay inside these ranges and needn't reach their ends.
All inputs are finite; a program needn't handle non-finite values.
Results may differ from the reference program's by a relative error of at most 0.011.
Values may be sent and summed in bfloat16 or wider, within the bound.
A program may use at most 64 MiB of HBM per device.

```python
import jax
import jax.numpy as jnp
from jax import lax

D = 2048
F = 4096
ROWS = 384
LAYERS = 4


def level_of(rng, extent, pieces, low, largest):
    def one(dim, blocks):
        steps = jax.random.uniform(jax.random.fold_in(jax.random.fold_in(rng, 6), dim), (blocks,), jnp.float32, low / len(pieces), largest / len(pieces))
        return jnp.repeat(jnp.exp(steps), extent[dim] // blocks).reshape((-1,) + (1,) * (len(extent) - dim - 1))

    loudness = one(*pieces[0])
    for cut in pieces[1:]:
        loudness = loudness * one(*cut)
    return loudness


def gaussian(rng, extent, deviation, most, pieces=(), held_as=jnp.bfloat16):
    gain = level_of(rng, extent, pieces, -0.22, 0.18) if pieces else 1.0
    values = jax.random.normal(rng, extent, jnp.float32) * deviation * gain
    return jnp.minimum(jnp.maximum(values, -most), most).astype(held_as)


def setup_inputs(seed: int = 0) -> dict:
    key_of = jax.random.split(jax.random.key(seed), 6)
    return {
        "layer_inputs": gaussian(key_of[0], (ROWS, LAYERS * D), 1.0, 6.0, ((0, 4), (1, 8))),
        "mlp_outputs": gaussian(key_of[1], (ROWS, LAYERS * D), 1.0, 6.0, ((0, 4), (1, 8))),
        "enc_weight": gaussian(key_of[2], (LAYERS * D, F), D ** -0.5, 0.125, ((0, 8), (1, 4))),
        "enc_bias": jnp.clip(-1.0 + 1.5 * jax.random.uniform(key_of[3], (LAYERS, F), jnp.float32) ** level_of(key_of[3], (LAYERS, F), ((1, 4),), -0.2, 0.2), -1.0, 0.5),
        "dec_weight": gaussian(key_of[4], (LAYERS, F, LAYERS * D), (LAYERS * F) ** -0.5, 0.046875, ((1, 4), (2, 8))),
    }


def reference(layer_inputs, mlp_outputs, enc_weight, enc_bias, dec_weight):
    rscale = ROWS ** -0.5
    pre_list = []
    latent_list = []
    for source in range(LAYERS):
        layer_in = layer_inputs[:, source * D:(source + 1) * D]
        pre_acts = jnp.dot(layer_in, enc_weight[source * D:(source + 1) * D], preferred_element_type=jnp.float32) + enc_bias[source][None, :]
        pre_list.append(pre_acts)
        latent_list.append(jnp.maximum(pre_acts, 0.0).astype(jnp.bfloat16))
    grad_list = []
    for target in range(LAYERS):
        recon = jnp.zeros((ROWS, D), jnp.float32)
        for source in range(target + 1):
            recon = recon + jnp.dot(latent_list[source], dec_weight[source, :, target * D:(target + 1) * D], preferred_element_type=jnp.float32)
        wanted = mlp_outputs[:, target * D:(target + 1) * D].astype(jnp.float32)
        grad_list.append(((recon - wanted) * rscale).astype(jnp.bfloat16))
    dec_rows = []
    enc_rows = []
    for source in range(LAYERS):
        blocks = []
        lat_grad = jnp.zeros((ROWS, F), jnp.float32)
        for target in range(LAYERS):
            if target >= source:
                piece = lax.dot_general(latent_list[source], grad_list[target], (((0,), (0,)), ((), ())), preferred_element_type=jnp.float32)
                blocks.append(piece.astype(jnp.bfloat16))
                weight = dec_weight[source, :, target * D:(target + 1) * D]
                lat_grad = lat_grad + lax.dot_general(grad_list[target], weight, (((1,), (1,)), ((), ())), preferred_element_type=jnp.float32)
            else:
                blocks.append(jnp.zeros((F, D), jnp.bfloat16))
        dec_rows.append(jnp.concatenate(blocks, axis=1))
        pre_grad = jnp.where(pre_list[source] > 0.0, lat_grad, 0.0).astype(jnp.bfloat16)
        layer_in = layer_inputs[:, source * D:(source + 1) * D]
        enc_rows.append(lax.dot_general(layer_in, pre_grad, (((0,), (0,)), ((), ())), preferred_element_type=jnp.float32))
    return jnp.concatenate(enc_rows, axis=0), jnp.stack(dec_rows, axis=0)
```

```python
import functools

import jax
import jax.numpy as jnp
from jax import lax
from jax.experimental import pallas as pl
from jax.experimental.pallas import tpu as pltpu
from jax.sharding import PartitionSpec as P

MESH = pl.DeviceIdType.MESH
F32 = jnp.float32
BF16 = jnp.bfloat16


def exchange_kernel(
    layers, blocks, rscale,
    x_ref, mlp_ref, w_hbm, bias_ref, v_hbm,
    lat_out, og_out, xg_out, pg_out,
    xg, w, v, part_send, part_recv, pre, lat, recon, rs_send, rs_recv, og,
    bys, byr, bown, bzs, bzr, pg,
    x_ss, x_rs, p_ss, p_rs, z_ss, z_rs, y_ss, y_rs, rs_ss, rs_rs, og_ss, og_fs, og_rs,
    by_ss, by_rs, bz_ss, bz_rs, f_ss, f_rs, w_sem, v_sem, lat_sem, out_sem,
):
    p = lax.axis_index("layer")
    q = lax.axis_index("latent")
    t = p // 2
    y = p % 2
    o = 1 - y
    rb, depth = x_ref.shape
    half = w.shape[1] // 2
    partner = (p + 1 - 2 * y, q)
    up = (p + 2, q)
    down = (p - 2, q)
    chips = blocks // 2

    def blk(k):
        return ((q // 2 + k // 2) % chips) * 2 + (q % 2 + k % 2) % 2

    def rows(b):
        return pl.ds(pl.multiple_of(b * rb, rb), rb)

    def cols(h):
        return pl.ds(pl.multiple_of(h * half, half), half)

    def rcopy(src, dst, ss, rs, dev):
        return pltpu.make_async_remote_copy(
            src_ref=src, dst_ref=dst, send_sem=ss, recv_sem=rs, device_id=dev, device_id_type=MESH
        )

    w_copy = pltpu.make_async_copy(w_hbm, w, w_sem)
    w_copy.start()
    v_copy = pltpu.make_async_copy(v_hbm, v, v_sem)
    v_copy.start()

    barrier = pltpu.get_barrier_semaphore()
    for k in range(1, blocks):
        pl.semaphore_signal(barrier, inc=1, device_id=(p, blk(k)), device_id_type=MESH)
    pl.semaphore_signal(barrier, inc=1, device_id=partner, device_id_type=MESH)

    @pl.when(t < layers - 1)
    def _():
        pl.semaphore_signal(barrier, inc=1, device_id=up, device_id_type=MESH)

    @pl.when(t > 0)
    def _():
        pl.semaphore_signal(barrier, inc=1, device_id=down, device_id_type=MESH)

    neighbours = blocks + (t < layers - 1).astype(jnp.int32) + (t > 0).astype(jnp.int32)
    pl.semaphore_wait(barrier, neighbours)

    def x_copy(k):
        return rcopy(x_ref, xg.at[rows(q)], x_ss.at[k], x_rs.at[q], (p, blk(k)))

    for k in list(range(2, blocks)) + [1]:
        x_copy(k).start()
    xg[rows(q), :] = x_ref[...]

    def part_copy(b):
        return rcopy(part_send.at[rows(b)], part_recv.at[rows(b)], p_ss.at[b], p_rs.at[b], partner)

    def lat_up(l, b):
        piece = lat.at[l, y, rows(b)]
        return rcopy(piece, piece, z_ss.at[l, b], z_rs.at[l, b], up)

    def lat_swap(l, b):
        piece = lat.at[l, y, rows(b)]
        return rcopy(piece, piece, y_ss.at[l, b], y_rs.at[l, b], partner)

    def lat_swap_in(l, b):
        piece = lat.at[l, o, rows(b)]
        return rcopy(piece, piece, y_ss.at[l, b], y_rs.at[l, b], partner)

    def own_block(b):
        part_copy(b).wait_recv()
        total = pre[rows(b), :] + part_recv[rows(b), :] + bias
        pre[rows(b), :] = total
        lat[t, y, rows(b), :] = jnp.maximum(total, 0.0).astype(BF16)

        @pl.when(t < layers - 1)
        def _():
            lat_up(t, b).start()

        lat_swap(t, b).start()

    bias_half = jnp.where(y == 0, bias_ref[:, :half], bias_ref[:, half:])
    own_row = lax.broadcasted_iota(jnp.int32, bias_half.shape, 0) == t
    bias = jnp.sum(jnp.where(own_row, bias_half, 0.0), axis=0, keepdims=True)
    w_copy.wait()
    for k in range(blocks):
        b = blk(k)
        if k > 0:
            rcopy(x_ref, xg.at[rows(b)], x_ss.at[k], x_rs.at[b], (p, b)).wait_recv()
        part_send[rows(b), :] = jnp.dot(xg[rows(b), :], w[:, cols(o)], preferred_element_type=F32)
        part_copy(b).start()
        pre[rows(b), :] = jnp.dot(xg[rows(b), :], w[:, cols(y)], preferred_element_type=F32)
        if k > 0:
            own_block(blk(k - 1))
    own_block(blk(blocks - 1))
    xg_copy = pltpu.make_async_copy(xg, xg_out, out_sem.at[0])
    xg_copy.start()

    recon[...] = jnp.zeros_like(recon)
    v_copy.wait()

    def decode(l, h):
        recon[...] += jnp.dot(lat[l, h], v[l, cols(h), :], preferred_element_type=F32)

    def forward(s, carry):
        l = t - s

        @pl.when(jnp.logical_and(s > 0, s <= t))
        def _():
            for k in range(blocks):
                b = blk(k)
                lat_up(l, b).wait_recv()

                @pl.when(t < layers - 1)
                def _():
                    lat_up(l, b).start()

                lat_swap(l, b).start()

        @pl.when(s <= t)
        def _():
            decode(l, y)

        @pl.when(s > 0)
        def _():
            for k in range(blocks):
                lat_swap_in(l + 1, blk(k)).wait_recv()
            decode(l + 1, o)

        return carry

    lax.fori_loop(0, t + 2, forward, 0)

    def rs_copy(k):
        return rcopy(rs_send.at[k], rs_recv.at[q], rs_ss.at[k], rs_rs.at[q], (p, blk(k)))

    order = list(range(2, blocks)) + [1]
    for k in order:
        rs_send[k] = recon[rows(blk(k)), :].astype(BF16)
        rs_copy(k).start()
    total = recon[rows(q), :]
    for k in order[-1:] + order[:-1]:
        b = blk(k)
        rcopy(rs_send.at[k], rs_recv.at[b], rs_ss.at[k], rs_rs.at[b], (p, b)).wait_recv()
        total = total + rs_recv[b].astype(F32)
    og[rows(q), :] = ((total - mlp_ref[...].astype(F32)) * rscale).astype(BF16)

    def og_copy(src, ss, k):
        return rcopy(og.at[rows(src)], og.at[rows(src)], ss.at[k], og_rs.at[src], (p, blk(k)))

    def og_relay(k):
        return rcopy(og.at[rows(blk(k))], og.at[rows(blk(k))], og_fs.at[k], og_rs.at[blk(k)], (p, blk(1)))

    for k in list(range(2, blocks, 2)) + [1]:
        og_copy(q, og_ss, k).start()
    for k in range(2, blocks, 2):
        og_copy(blk(k), og_ss, k).wait_recv()
        og_relay(k).start()
    for k in range(1, blocks, 2):
        og_copy(blk(k), og_ss, k).wait_recv()
    og_dma = pltpu.make_async_copy(og, og_out, out_sem.at[1])
    og_dma.start()

    def lat_dma(l):
        return pltpu.make_async_copy(lat.at[l], lat_out.at[l], lat_sem.at[l])

    def by_copy(l, b):
        return rcopy(bys.at[l, rows(b)], byr.at[l, rows(b)], by_ss.at[l, b], by_rs.at[l, b], partner)

    def bz_copy(l, b):
        return rcopy(bzs.at[l, rows(b)], bzr.at[l, rows(b)], bz_ss.at[l, b], bz_rs.at[l, b], down)

    def back(l, h):
        return lax.dot_general(
            og[...], v[l, cols(h), :], (((1,), (1,)), ((), ())), preferred_element_type=F32
        )

    def produce(l, carry):
        bys[l] = back(l, o).astype(BF16)
        for b in range(blocks):
            by_copy(l, b).start()
        bown[l] = back(l, y)
        lat_dma(l).start()
        return carry

    lax.fori_loop(0, t + 1, produce, 0)

    def collected(l, b):
        by_copy(l, b).wait_recv()

        @pl.when(t < layers - 1)
        def _():
            bz_copy(l, b).wait_recv()
            bown[l, rows(b), :] += bzr[l, rows(b), :].astype(F32)

        return bown[l, rows(b), :] + byr[l, rows(b), :].astype(F32)

    def combine(l, carry):
        for b in range(blocks):
            bzs[l, rows(b), :] = collected(l, b).astype(BF16)
            bz_copy(l, b).start()
        return carry

    lax.fori_loop(0, t, combine, 0)

    def final_copy(h, b):
        piece = pg.at[h, rows(b)]
        return rcopy(piece, piece, f_ss.at[b], f_rs.at[b], partner)

    for b in range(blocks):
        value = jnp.where(pre[rows(b), :] > 0.0, collected(t, b), 0.0)
        pg[y, rows(b), :] = value.astype(BF16)
        final_copy(y, b).start()
    for b in range(blocks):
        final_copy(o, b).wait_recv()
    pg_dma = pltpu.make_async_copy(pg, pg_out, out_sem.at[2])
    pg_dma.start()

    for k in range(1, blocks):
        x_copy(k).wait_send()
        rs_copy(k).wait_send()
    for k in list(range(2, blocks, 2)) + [1]:
        og_copy(q, og_ss, k).wait_send()
    for k in range(2, blocks, 2):
        og_relay(k).wait_send()
    for b in range(blocks):
        part_copy(b).wait_send()
        final_copy(y, b).wait_send()

    def drain(l, carry):
        lat_dma(l).wait()
        for b in range(blocks):
            lat_swap(l, b).wait_send()
            by_copy(l, b).wait_send()

            @pl.when(t < layers - 1)
            def _():
                lat_up(l, b).wait_send()

            @pl.when(l < t)
            def _():
                bz_copy(l, b).wait_send()

        return carry

    lax.fori_loop(0, t + 1, drain, 0)
    xg_copy.wait()
    og_dma.wait()
    pg_dma.wait()


def exchange(layer_inputs, mlp_outputs, enc_weight, enc_bias, dec_weight):
    layers, latents, width = dec_weight.shape
    blocks = lax.axis_size("latent")
    rb, depth = layer_inputs.shape
    total_rows = rb * blocks
    half = latents // 2
    rscale = total_rows ** (-0.5)
    vmem = pl.BlockSpec(memory_space=pltpu.VMEM)
    anywhere = pl.BlockSpec(memory_space=pl.ANY)
    dma = pltpu.SemaphoreType.DMA
    per_block = dma((blocks,))
    per_layer = dma((layers, blocks))
    return pl.pallas_call(
        functools.partial(exchange_kernel, layers, blocks, rscale),
        out_shape=(
            jax.ShapeDtypeStruct((layers, 2, total_rows, half), BF16),
            jax.ShapeDtypeStruct((total_rows, width), BF16),
            jax.ShapeDtypeStruct((total_rows, depth), BF16),
            jax.ShapeDtypeStruct((2, total_rows, half), BF16),
        ),
        in_specs=[vmem, vmem, anywhere, vmem, anywhere],
        out_specs=(anywhere,) * 4,
        scratch_shapes=[
            pltpu.VMEM((total_rows, depth), BF16),
            pltpu.VMEM((depth, latents), BF16),
            pltpu.VMEM((layers, latents, width), BF16),
            pltpu.VMEM((total_rows, half), F32),
            pltpu.VMEM((total_rows, half), F32),
            pltpu.VMEM((total_rows, half), F32),
            pltpu.VMEM((layers, 2, total_rows, half), BF16),
            pltpu.VMEM((total_rows, width), F32),
            pltpu.VMEM((blocks, rb, width), BF16),
            pltpu.VMEM((blocks, rb, width), BF16),
            pltpu.VMEM((total_rows, width), BF16),
            pltpu.VMEM((layers, total_rows, half), BF16),
            pltpu.VMEM((layers, total_rows, half), BF16),
            pltpu.VMEM((layers, total_rows, half), F32),
            pltpu.VMEM((layers, total_rows, half), BF16),
            pltpu.VMEM((layers, total_rows, half), BF16),
            pltpu.VMEM((2, total_rows, half), BF16),
            per_block, per_block, per_block, per_block,
            per_layer, per_layer, per_layer, per_layer,
            per_block, per_block, per_block, per_block, per_block,
            per_layer, per_layer, per_layer, per_layer,
            per_block, per_block,
            dma, dma, dma((layers,)), dma((3,)),
        ],
        compiler_params=pltpu.CompilerParams(
            collective_id=0, has_side_effects=True, vmem_limit_bytes=48 * 2**20
        ),
        name="exchange",
    )(layer_inputs, mlp_outputs, enc_weight, enc_bias, dec_weight)


def transposed_dot(a, b):
    return lax.dot_general(a, b, (((0,), (0,)), ((), ())), preferred_element_type=F32)


def dec_kernel(lat_ref, og_ref, out_ref):
    layer_now = lax.axis_index("layer") // 2
    source = pl.program_id(0)

    @pl.when(source <= layer_now)
    def _():
        out_ref[0] = transposed_dot(lat_ref[0, 0], og_ref[...]).astype(BF16)

    @pl.when(source > layer_now)
    def _():
        out_ref[...] = jnp.zeros_like(out_ref)


def enc_kernel(x_ref, pg_ref, out_ref):
    out_ref[...] = transposed_dot(x_ref[...], pg_ref[0])


def local(layer_inputs, mlp_outputs, enc_weight, enc_bias, dec_weight):
    lat, og, xg, pg = exchange(layer_inputs, mlp_outputs, enc_weight, enc_bias, dec_weight)
    layers, _, total_rows, half = lat.shape
    width = og.shape[1]
    depth = xg.shape[1]
    dec_grad = pl.pallas_call(
        dec_kernel,
        grid=(layers, 2),
        in_specs=[
            pl.BlockSpec((1, 1, total_rows, half), lambda l, h: (l, h, 0, 0)),
            pl.BlockSpec((total_rows, width), lambda l, h: (0, 0)),
        ],
        out_specs=pl.BlockSpec((1, half, width), lambda l, h: (l, h, 0)),
        out_shape=jax.ShapeDtypeStruct(dec_weight.shape, BF16),
        name="dec_grad",
    )(lat, og)
    enc_grad = pl.pallas_call(
        enc_kernel,
        grid=(2, 2),
        in_specs=[
            pl.BlockSpec((total_rows, depth // 2), lambda h, i: (0, i)),
            pl.BlockSpec((1, total_rows, half), lambda h, i: (h, 0, 0)),
        ],
        out_specs=pl.BlockSpec((depth // 2, half), lambda h, i: (i, h)),
        out_shape=jax.ShapeDtypeStruct(enc_weight.shape, F32),
        name="enc_grad",
    )(xg, pg)
    return (enc_grad, dec_grad)


def solution(mesh):
    in_specs = (
        P("latent", "layer"),
        P("latent", "layer"),
        P("layer", "latent"),
        P(None, "latent"),
        P(None, "latent", "layer"),
    )
    out_specs = (P("layer", "latent"), P(None, "latent", "layer"))
    return jax.shard_map(local, mesh=mesh, in_specs=in_specs, out_specs=out_specs, check_vma=False)
```

```python
import functools

import jax
import jax.numpy as jnp
from jax import lax
from jax.experimental import pallas as pl
from jax.experimental.pallas import tpu as pltpu
from jax.sharding import PartitionSpec as P

MESH = pl.DeviceIdType.MESH
F32 = jnp.float32
BF16 = jnp.bfloat16


def exchange_kernel(
    layers, blocks, rscale,
    x_hbm, mlp_hbm, w_hbm, bias_hbm, v_hbm,
    dec_out, xg_out, pg_out,
    xg, mlp, w, bias_all, v, part_send, part_recv, pre, lat, recon, rs_send, rs_recv, og,
    bys, byr, bown, bof, bzs, bzr, bzso, bzro, pg, dec,
    x_ss, x_rs, p_ss, p_rs, z_ss, z_rs, zo_ss, zo_rs, y_ss, y_rs, rs_ss, rs_rs, og_ss, og_fs, og_rs,
    by_ss, by_rs, bz_ss, bz_rs, bzo_ss, bzo_rs, f_ss, f_rs, in_sem, dec_sem, out_sem,
):
    p = lax.axis_index("layer")
    q = lax.axis_index("latent")
    t = p // 2
    y = p % 2
    o = 1 - y
    rb = x_hbm.shape[0]
    half = w.shape[1] // 2
    partner = (p + 1 - 2 * y, q)
    up = (p + 2, q)
    down = (p - 2, q)
    chips = blocks // 2

    def blk(k):
        return ((q // 2 + k // 2) % chips) * 2 + (q % 2 + k % 2) % 2

    def rows(b):
        return pl.ds(pl.multiple_of(b * rb, rb), rb)

    def cols(h):
        return pl.ds(pl.multiple_of(h * half, half), half)

    def rcopy(src, dst, ss, rs, dev):
        return pltpu.make_async_remote_copy(
            src_ref=src, dst_ref=dst, send_sem=ss, recv_sem=rs, device_id=dev, device_id_type=MESH
        )

    own_x = pltpu.make_async_copy(x_hbm, xg.at[rows(q)], in_sem.at[0])
    w_copy = pltpu.make_async_copy(w_hbm, w, in_sem.at[1])
    bias_copy = pltpu.make_async_copy(bias_hbm, bias_all, in_sem.at[2])
    mlp_copy = pltpu.make_async_copy(mlp_hbm, mlp, in_sem.at[3])
    v_copy = pltpu.make_async_copy(v_hbm, v, in_sem.at[4])
    for copy in (own_x, w_copy, bias_copy, mlp_copy, v_copy):
        copy.start()
    both_up = list(range(blocks // 2, blocks))
    one_up = list(range(blocks // 2))
    both_down = list(range(blocks - max(blocks // 4, 1), blocks))
    one_down = list(range(blocks - max(blocks // 4, 1)))

    barrier = pltpu.get_barrier_semaphore()
    for k in range(1, blocks):
        pl.semaphore_signal(barrier, inc=1, device_id=(p, blk(k)), device_id_type=MESH)
    pl.semaphore_signal(barrier, inc=1, device_id=partner, device_id_type=MESH)

    @pl.when(t < layers - 1)
    def _():
        pl.semaphore_signal(barrier, inc=1, device_id=up, device_id_type=MESH)

    @pl.when(t > 0)
    def _():
        pl.semaphore_signal(barrier, inc=1, device_id=down, device_id_type=MESH)

    neighbours = blocks + (t < layers - 1).astype(jnp.int32) + (t > 0).astype(jnp.int32)
    pl.semaphore_wait(barrier, neighbours)

    def x_copy(k):
        return rcopy(x_hbm, xg.at[rows(q)], x_ss.at[k], x_rs.at[q], (p, blk(k)))

    for k in list(range(2, blocks)) + [1]:
        x_copy(k).start()

    def part_copy(b):
        return rcopy(part_send.at[rows(b)], part_recv.at[rows(b)], p_ss.at[b], p_rs.at[b], partner)

    def lat_up(l, b):
        piece = lat.at[l, y, rows(b)]
        return rcopy(piece, piece, z_ss.at[l, b], z_rs.at[l, b], up)

    def lat_up_other(l, b):
        piece = lat.at[l, o, rows(b)]
        return rcopy(piece, piece, zo_ss.at[l, b], zo_rs.at[l, b], up)

    def lat_swap(l, b):
        piece = lat.at[l, y, rows(b)]
        return rcopy(piece, piece, y_ss.at[l, b], y_rs.at[l, b], partner)

    def lat_swap_in(l, b):
        piece = lat.at[l, o, rows(b)]
        return rcopy(piece, piece, y_ss.at[l, b], y_rs.at[l, b], partner)

    def own_block(b):
        part_copy(b).wait_recv()
        total = pre[rows(b), :] + part_recv[rows(b), :] + bias
        pre[rows(b), :] = total
        lat[t, y, rows(b), :] = jnp.maximum(total, 0.0).astype(BF16)

        @pl.when(t < layers - 1)
        def _():
            lat_up(t, b).start()

        lat_swap(t, b).start()

    bias_copy.wait()
    bias_half = jnp.where(y == 0, bias_all[:, :half], bias_all[:, half:])
    own_row = lax.broadcasted_iota(jnp.int32, bias_half.shape, 0) == t
    bias = jnp.sum(jnp.where(own_row, bias_half, 0.0), axis=0, keepdims=True)
    own_x.wait()
    w_copy.wait()
    for k in range(blocks):
        b = blk(k)
        if k > 0:
            rcopy(x_hbm, xg.at[rows(b)], x_ss.at[k], x_rs.at[b], (p, b)).wait_recv()
        part_send[rows(b), :] = jnp.dot(xg[rows(b), :], w[:, cols(o)], preferred_element_type=F32)
        part_copy(b).start()
        pre[rows(b), :] = jnp.dot(xg[rows(b), :], w[:, cols(y)], preferred_element_type=F32)
        if k > 0:
            own_block(blk(k - 1))
    own_block(blk(blocks - 1))
    xg_copy = pltpu.make_async_copy(xg, xg_out, out_sem.at[0])
    xg_copy.start()

    recon[...] = jnp.zeros_like(recon)
    v_copy.wait()

    def decode(l, h):
        recon[...] += jnp.dot(lat[l, h], v[l, cols(h), :], preferred_element_type=F32)

    def other_up(l, b):
        @pl.when(t < layers - 1)
        def _():
            lat_up_other(l, b).start()

    for k in both_up:
        b = blk(k)
        lat_swap_in(t, b).wait_recv()
        other_up(t, b)

    def forward(s, carry):
        l = t - s

        @pl.when(jnp.logical_and(s > 0, s <= t))
        def _():
            for k in range(blocks):
                b = blk(k)
                lat_up(l, b).wait_recv()

                @pl.when(t < layers - 1)
                def _():
                    lat_up(l, b).start()

                if k in one_up:
                    lat_swap(l, b).start()
            for k in both_up:
                b = blk(k)
                lat_up_other(l, b).wait_recv()
                other_up(l, b)

        @pl.when(s <= t)
        def _():
            decode(l, y)

        @pl.when(s > 0)
        def _():
            for k in one_up:
                lat_swap_in(l + 1, blk(k)).wait_recv()
            decode(l + 1, o)

        return carry

    lax.fori_loop(0, t + 2, forward, 0)

    def rs_copy(k):
        return rcopy(rs_send.at[k], rs_recv.at[q], rs_ss.at[k], rs_rs.at[q], (p, blk(k)))

    mlp_copy.wait()
    order = list(range(2, blocks)) + [1]
    for k in order:
        rs_send[k] = recon[rows(blk(k)), :].astype(BF16)
        rs_copy(k).start()
    total = recon[rows(q), :]
    for k in order[-1:] + order[:-1]:
        b = blk(k)
        rcopy(rs_send.at[k], rs_recv.at[b], rs_ss.at[k], rs_rs.at[b], (p, b)).wait_recv()
        total = total + rs_recv[b].astype(F32)
    og[rows(q), :] = ((total - mlp[...].astype(F32)) * rscale).astype(BF16)

    def og_copy(src, ss, k):
        return rcopy(og.at[rows(src)], og.at[rows(src)], ss.at[k], og_rs.at[src], (p, blk(k)))

    def og_relay(k):
        return rcopy(og.at[rows(blk(k))], og.at[rows(blk(k))], og_fs.at[k], og_rs.at[blk(k)], (p, blk(1)))

    for k in list(range(2, blocks, 2)) + [1]:
        og_copy(q, og_ss, k).start()
    for k in range(2, blocks, 2):
        og_copy(blk(k), og_ss, k).wait_recv()
        og_relay(k).start()
    for k in range(1, blocks, 2):
        og_copy(blk(k), og_ss, k).wait_recv()

    def by_copy(l, b):
        return rcopy(bys.at[l, rows(b)], byr.at[l, rows(b)], by_ss.at[l, b], by_rs.at[l, b], partner)

    def bz_copy(l, b):
        return rcopy(bzs.at[l, rows(b)], bzr.at[l, rows(b)], bz_ss.at[l, b], bz_rs.at[l, b], down)

    def bz_other(l, b):
        return rcopy(bzso.at[l, rows(b)], bzro.at[l, rows(b)], bzo_ss.at[l, b], bzo_rs.at[l, b], down)

    def dec_copy(l):
        return pltpu.make_async_copy(dec.at[l], dec_out.at[l], dec_sem.at[l])

    def back(l, h):
        return lax.dot_general(
            og[...], v[l, cols(h), :], (((1,), (1,)), ((), ())), preferred_element_type=F32
        )

    def add_own(l, b):
        bz_copy(l, b).wait_recv()
        bown[l, rows(b), :] += bzr[l, rows(b), :].astype(F32)

    def add_other(l, b):
        bz_other(l, b).wait_recv()
        bof[l, rows(b), :] += bzro[l, rows(b), :].astype(F32)

    def send_both(l, b):
        bzs[l, rows(b), :] = bown[l, rows(b), :].astype(BF16)
        bz_copy(l, b).start()
        bzso[l, rows(b), :] = bof[l, rows(b), :].astype(BF16)
        bz_other(l, b).start()

    def swap_sum(l, b):
        bys[l, rows(b), :] = bof[l, rows(b), :].astype(BF16)
        by_copy(l, b).start()

    def produce(l, carry):
        bof[l] = back(l, o)
        for k in one_down:
            swap_sum(l, blk(k))
        bown[l] = back(l, y)

        @pl.when(t == layers - 1)
        def _():
            for k in both_down:
                b = blk(k)

                @pl.when(l < t)
                def _():
                    send_both(l, b)

                @pl.when(l == t)
                def _():
                    swap_sum(l, b)

        return carry

    lax.fori_loop(0, t + 1, produce, 0)

    def collected(l, b):
        by_copy(l, b).wait_recv()
        return bown[l, rows(b), :] + byr[l, rows(b), :].astype(F32)

    def dec_piece(l):
        for h in range(2):
            piece = lax.dot_general(
                lat[l, h], og[...], (((0,), (0,)), ((), ())), preferred_element_type=F32
            )
            dec[l, h * half:(h + 1) * half, :] = piece.astype(BF16)
        dec_copy(l).start()

    def combine(l, carry):
        @pl.when(l < t)
        def _():
            @pl.when(t < layers - 1)
            def _():
                for k in both_down:
                    b = blk(k)
                    add_own(l, b)
                    add_other(l, b)
                    send_both(l, b)

            for k in one_down:
                b = blk(k)

                @pl.when(t < layers - 1)
                def _():
                    add_own(l, b)

                bzs[l, rows(b), :] = collected(l, b).astype(BF16)
                bz_copy(l, b).start()

        dec_piece(l)
        return carry

    lax.fori_loop(0, t + 1, combine, 0)

    def final_copy(h, b):
        piece = pg.at[h, rows(b)]
        return rcopy(piece, piece, f_ss.at[b], f_rs.at[b], partner)

    @pl.when(t < layers - 1)
    def _():
        for k in both_down:
            b = blk(k)
            add_own(t, b)
            add_other(t, b)
            swap_sum(t, b)

    for k in one_down + both_down:
        b = blk(k)
        if k in one_down:
            @pl.when(t < layers - 1)
            def _():
                add_own(t, b)

        value = jnp.where(pre[rows(b), :] > 0.0, collected(t, b), 0.0)
        pg[y, rows(b), :] = value.astype(BF16)
        final_copy(y, b).start()
    for b in range(blocks):
        final_copy(o, b).wait_recv()
    pg_dma = pltpu.make_async_copy(pg, pg_out, out_sem.at[1])
    pg_dma.start()

    for k in range(1, blocks):
        x_copy(k).wait_send()
        rs_copy(k).wait_send()
    for k in list(range(2, blocks, 2)) + [1]:
        og_copy(q, og_ss, k).wait_send()
    for k in range(2, blocks, 2):
        og_relay(k).wait_send()
    for b in range(blocks):
        part_copy(b).wait_send()
        final_copy(y, b).wait_send()

    def drain(l, carry):
        dec_copy(l).wait()
        for k in range(blocks):
            b = blk(k)

            @pl.when(jnp.logical_or(l == t, k in one_up))
            def _():
                lat_swap(l, b).wait_send()

            @pl.when(jnp.logical_or(l == t, k in one_down))
            def _():
                by_copy(l, b).wait_send()

            @pl.when(t < layers - 1)
            def _():
                lat_up(l, b).wait_send()
                if k in both_up:
                    lat_up_other(l, b).wait_send()

            @pl.when(l < t)
            def _():
                bz_copy(l, b).wait_send()
                if k in both_down:
                    bz_other(l, b).wait_send()

        return carry

    lax.fori_loop(0, t + 1, drain, 0)
    xg_copy.wait()
    pg_dma.wait()


def exchange(layer_inputs, mlp_outputs, enc_weight, enc_bias, dec_weight):
    layers, latents, width = dec_weight.shape
    blocks = lax.axis_size("latent")
    rb, depth = layer_inputs.shape
    total_rows = rb * blocks
    half = latents // 2
    rscale = total_rows ** (-0.5)
    hbm = pl.BlockSpec(memory_space=pltpu.HBM)
    dma = pltpu.SemaphoreType.DMA
    per_block = dma((blocks,))
    per_layer = dma((layers, blocks))
    sums = pltpu.VMEM((layers, total_rows, half), F32)
    sent = pltpu.VMEM((layers, total_rows, half), BF16)
    one_half = pltpu.VMEM((total_rows, half), F32)
    row_blocks = pltpu.VMEM((blocks, rb, width), BF16)
    return pl.pallas_call(
        functools.partial(exchange_kernel, layers, blocks, rscale),
        out_shape=(
            jax.ShapeDtypeStruct((layers, latents, width), BF16),
            jax.ShapeDtypeStruct((total_rows, depth), BF16),
            jax.ShapeDtypeStruct((2, total_rows, half), BF16),
        ),
        in_specs=[hbm] * 5,
        out_specs=(hbm,) * 3,
        scratch_shapes=[
            pltpu.VMEM((total_rows, depth), BF16),
            pltpu.VMEM((rb, width), BF16),
            pltpu.VMEM((depth, latents), BF16),
            pltpu.VMEM((layers, latents), F32),
            pltpu.VMEM((layers, latents, width), BF16),
            one_half, one_half, one_half,
            pltpu.VMEM((layers, 2, total_rows, half), BF16),
            pltpu.VMEM((total_rows, width), F32),
            row_blocks, row_blocks,
            pltpu.VMEM((total_rows, width), BF16),
            sent, sent, sums, sums, sent, sent, sent, sent,
            pltpu.VMEM((2, total_rows, half), BF16),
            pltpu.VMEM((layers, latents, width), BF16),
            per_block, per_block, per_block, per_block,
            per_layer, per_layer, per_layer, per_layer, per_layer, per_layer,
            per_block, per_block, per_block, per_block, per_block,
            per_layer, per_layer, per_layer, per_layer, per_layer, per_layer,
            per_block, per_block,
            dma((5,)), dma((layers,)), dma((2,)),
        ],
        compiler_params=pltpu.CompilerParams(
            collective_id=0, has_side_effects=True, vmem_limit_bytes=56 * 2**20
        ),
        name="exchange",
    )(layer_inputs, mlp_outputs, enc_weight, enc_bias, dec_weight)


def transposed_dot(a, b):
    return lax.dot_general(a, b, (((0,), (0,)), ((), ())), preferred_element_type=F32)


def finish_kernel(x_ref, pg_ref, dec_ref, enc_out, dec_out):
    layer_now = lax.axis_index("layer") // 2
    source = pl.program_id(1)
    enc_out[...] = transposed_dot(x_ref[...], pg_ref[0])

    @pl.when(source <= layer_now)
    def _():
        dec_out[...] = dec_ref[...]

    @pl.when(source > layer_now)
    def _():
        dec_out[...] = jnp.zeros_like(dec_out)


def local(layer_inputs, mlp_outputs, enc_weight, enc_bias, dec_weight):
    dec, xg, pg = exchange(layer_inputs, mlp_outputs, enc_weight, enc_bias, dec_weight)
    layers, latents, width = dec.shape
    total_rows, depth = xg.shape
    half = latents // 2
    piece = depth // layers
    return pl.pallas_call(
        finish_kernel,
        grid=(2, layers),
        in_specs=[
            pl.BlockSpec((total_rows, piece), lambda h, l: (0, l)),
            pl.BlockSpec((1, total_rows, half), lambda h, l: (h, 0, 0)),
            pl.BlockSpec((1, half, width), lambda h, l: (l, h, 0)),
        ],
        out_specs=(
            pl.BlockSpec((piece, half), lambda h, l: (l, h)),
            pl.BlockSpec((1, half, width), lambda h, l: (l, h, 0)),
        ),
        out_shape=(
            jax.ShapeDtypeStruct(enc_weight.shape, F32),
            jax.ShapeDtypeStruct(dec_weight.shape, BF16),
        ),
        name="finish",
    )(xg, pg, dec)


def solution(mesh):
    in_specs = (
        P("latent", "layer"),
        P("latent", "layer"),
        P("layer", "latent"),
        P(None, "latent"),
        P(None, "latent", "layer"),
    )
    out_specs = (P("layer", "latent"), P(None, "latent", "layer"))
    return jax.shard_map(local, mesh=mesh, in_specs=in_specs, out_specs=out_specs, check_vma=False)
```

```python
import functools

import jax
import jax.numpy as jnp
from jax import lax
from jax.experimental import pallas as pl
from jax.experimental.pallas import tpu as pltpu
from jax.sharding import PartitionSpec as P

MESH = pl.DeviceIdType.MESH
F32 = jnp.float32
BF16 = jnp.bfloat16


def exchange_kernel(
    layers, blocks, rscale,
    x_hbm, mlp_hbm, w_hbm, bias_hbm, v_hbm,
    dec_out, xg_out, pg_out,
    xg, mlp, w, bias_all, v, part_send, part_recv, pre, lat, recon, core_send, core_recv, rs_send, rs_recv, og,
    bys, byr, bown, bof, bzs, bzr, bzso, bzro, pg, dec,
    x_ss, x_rs, p_ss, p_rs, z_ss, z_rs, zo_ss, zo_rs, y_ss, y_rs, core_ss, core_rs, rs_ss, rs_rs, og_ss, og_fs, og_rs,
    by_ss, by_rs, bz_ss, bz_rs, bzo_ss, bzo_rs, f_ss, f_rs, in_sem, dec_sem, out_sem,
):
    p = lax.axis_index("layer")
    q = lax.axis_index("latent")
    t = p // 2
    y = p % 2
    o = 1 - y
    rb = x_hbm.shape[0]
    half = w.shape[1] // 2
    partner = (p + 1 - 2 * y, q)
    up = (p + 2, q)
    down = (p - 2, q)
    chips = blocks // 2

    def blk(k):
        return ((q // 2 + k // 2) % chips) * 2 + (q % 2 + k % 2) % 2

    def rows(b):
        return pl.ds(pl.multiple_of(b * rb, rb), rb)

    def cols(h):
        return pl.ds(pl.multiple_of(h * half, half), half)

    def rcopy(src, dst, ss, rs, dev):
        return pltpu.make_async_remote_copy(
            src_ref=src, dst_ref=dst, send_sem=ss, recv_sem=rs, device_id=dev, device_id_type=MESH
        )

    own_x = pltpu.make_async_copy(x_hbm, xg.at[rows(q)], in_sem.at[0])
    w_copy = pltpu.make_async_copy(w_hbm, w, in_sem.at[1])
    bias_copy = pltpu.make_async_copy(bias_hbm, bias_all, in_sem.at[2])
    mlp_copy = pltpu.make_async_copy(mlp_hbm, mlp, in_sem.at[3])
    v_copy = pltpu.make_async_copy(v_hbm, v, in_sem.at[4])
    for copy in (own_x, w_copy, bias_copy, mlp_copy, v_copy):
        copy.start()
    both_up = list(range(blocks // 2, blocks))
    one_up = list(range(blocks // 2))
    both_down = list(range(blocks - max(blocks // 4, 1), blocks))
    one_down = list(range(blocks - max(blocks // 4, 1)))

    barrier = pltpu.get_barrier_semaphore()
    for k in range(1, blocks):
        pl.semaphore_signal(barrier, inc=1, device_id=(p, blk(k)), device_id_type=MESH)
    pl.semaphore_signal(barrier, inc=1, device_id=partner, device_id_type=MESH)

    @pl.when(t < layers - 1)
    def _():
        pl.semaphore_signal(barrier, inc=1, device_id=up, device_id_type=MESH)

    @pl.when(t > 0)
    def _():
        pl.semaphore_signal(barrier, inc=1, device_id=down, device_id_type=MESH)

    neighbours = blocks + (t < layers - 1).astype(jnp.int32) + (t > 0).astype(jnp.int32)
    pl.semaphore_wait(barrier, neighbours)

    def x_copy(k):
        return rcopy(x_hbm, xg.at[rows(q)], x_ss.at[k], x_rs.at[q], (p, blk(k)))

    for k in list(range(2, blocks)) + [1]:
        x_copy(k).start()

    def part_copy(b):
        return rcopy(part_send.at[rows(b)], part_recv.at[rows(b)], p_ss.at[b], p_rs.at[b], partner)

    def lat_up(l, b):
        piece = lat.at[l, y, rows(b)]
        return rcopy(piece, piece, z_ss.at[l, b], z_rs.at[l, b], up)

    def lat_up_other(l, b):
        piece = lat.at[l, o, rows(b)]
        return rcopy(piece, piece, zo_ss.at[l, b], zo_rs.at[l, b], up)

    def lat_swap(l, b):
        piece = lat.at[l, y, rows(b)]
        return rcopy(piece, piece, y_ss.at[l, b], y_rs.at[l, b], partner)

    def lat_swap_in(l, b):
        piece = lat.at[l, o, rows(b)]
        return rcopy(piece, piece, y_ss.at[l, b], y_rs.at[l, b], partner)

    def own_block(b):
        part_copy(b).wait_recv()
        total = pre[rows(b), :] + part_recv[rows(b), :] + bias
        pre[rows(b), :] = total
        lat[t, y, rows(b), :] = jnp.maximum(total, 0.0).astype(BF16)

        @pl.when(t < layers - 1)
        def _():
            lat_up(t, b).start()

        lat_swap(t, b).start()

    bias_copy.wait()
    bias_half = jnp.where(y == 0, bias_all[:, :half], bias_all[:, half:])
    own_row = lax.broadcasted_iota(jnp.int32, bias_half.shape, 0) == t
    bias = jnp.sum(jnp.where(own_row, bias_half, 0.0), axis=0, keepdims=True)
    own_x.wait()
    w_copy.wait()
    for k in range(blocks):
        b = blk(k)
        if k > 0:
            rcopy(x_hbm, xg.at[rows(b)], x_ss.at[k], x_rs.at[b], (p, b)).wait_recv()
        part_send[rows(b), :] = jnp.dot(xg[rows(b), :], w[:, cols(o)], preferred_element_type=F32)
        part_copy(b).start()
        pre[rows(b), :] = jnp.dot(xg[rows(b), :], w[:, cols(y)], preferred_element_type=F32)
        if k > 0:
            own_block(blk(k - 1))
    own_block(blk(blocks - 1))
    xg_copy = pltpu.make_async_copy(xg, xg_out, out_sem.at[0])
    xg_copy.start()

    recon[...] = jnp.zeros_like(recon)
    v_copy.wait()

    def decode(l, h):
        recon[...] += jnp.dot(lat[l, h], v[l, cols(h), :], preferred_element_type=F32)

    def other_up(l, b):
        @pl.when(t < layers - 1)
        def _():
            lat_up_other(l, b).start()

    def forward(s, carry):
        l = t - s

        @pl.when(jnp.logical_and(s > 0, s <= t))
        def _():
            for k in range(blocks):
                b = blk(k)
                lat_up(l, b).wait_recv()

                @pl.when(t < layers - 1)
                def _():
                    lat_up(l, b).start()

                if k in one_up:
                    lat_swap(l, b).start()

        @pl.when(s <= t)
        def _():
            decode(l, y)

        @pl.when(s > 0)
        def _():
            for k in both_up:
                b = blk(k)

                @pl.when(s == 1)
                def _():
                    lat_swap_in(t, b).wait_recv()

                @pl.when(s > 1)
                def _():
                    lat_up_other(l + 1, b).wait_recv()

                other_up(l + 1, b)
            for k in one_up:
                lat_swap_in(l + 1, blk(k)).wait_recv()
            decode(l + 1, o)

        return carry

    lax.fori_loop(0, t + 2, forward, 0)

    def core_copy(c):
        return rcopy(core_send.at[c], core_recv.at[c], core_ss.at[c], core_rs.at[c], (p, blk(1)))

    def rs_copy(c):
        return rcopy(rs_send.at[c], rs_recv.at[q // 2], rs_ss.at[c], rs_rs.at[q // 2], (p, blk(2 * c)))

    def rs_in(c):
        chip = (q // 2 + c) % chips
        return rcopy(rs_send.at[c], rs_recv.at[chip], rs_ss.at[c], rs_rs.at[chip], (p, blk(2 * c)))

    order = list(range(1, chips)) + [0]
    for c in order:
        core_send[c] = recon[rows(blk(2 * c + 1)), :].astype(BF16)
        core_copy(c).start()
    for c in order:
        core_copy(c).wait_recv()
        total = recon[rows(blk(2 * c)), :] + core_recv[c].astype(F32)
        if c > 0:
            rs_send[c] = total.astype(BF16)
            rs_copy(c).start()
    mlp_copy.wait()
    for c in range(1, chips):
        rs_in(c).wait_recv()
        total = total + rs_recv[(q // 2 + c) % chips].astype(F32)
    og[rows(q), :] = ((total - mlp[...].astype(F32)) * rscale).astype(BF16)

    def og_copy(src, ss, k):
        return rcopy(og.at[rows(src)], og.at[rows(src)], ss.at[k], og_rs.at[src], (p, blk(k)))

    def og_relay(k):
        return rcopy(og.at[rows(blk(k))], og.at[rows(blk(k))], og_fs.at[k], og_rs.at[blk(k)], (p, blk(1)))

    for k in list(range(2, blocks, 2)) + [1]:
        og_copy(q, og_ss, k).start()
    for k in range(2, blocks, 2):
        og_copy(blk(k), og_ss, k).wait_recv()
        og_relay(k).start()
    for k in range(1, blocks, 2):
        og_copy(blk(k), og_ss, k).wait_recv()

    def by_copy(l, b):
        return rcopy(bys.at[l, rows(b)], byr.at[l, rows(b)], by_ss.at[l, b], by_rs.at[l, b], partner)

    def bz_copy(l, b):
        return rcopy(bzs.at[l, rows(b)], bzr.at[l, rows(b)], bz_ss.at[l, b], bz_rs.at[l, b], down)

    def bz_other(l, b):
        return rcopy(bzso.at[l, rows(b)], bzro.at[l, rows(b)], bzo_ss.at[l, b], bzo_rs.at[l, b], down)

    def dec_copy(l):
        return pltpu.make_async_copy(dec.at[l], dec_out.at[l], dec_sem.at[l])

    def back(l, h):
        return lax.dot_general(
            og[...], v[l, cols(h), :], (((1,), (1,)), ((), ())), preferred_element_type=F32
        )

    def add_own(l, b):
        bz_copy(l, b).wait_recv()
        bown[l, rows(b), :] += bzr[l, rows(b), :].astype(F32)

    def add_other(l, b):
        bz_other(l, b).wait_recv()
        bof[l, rows(b), :] += bzro[l, rows(b), :].astype(F32)

    def send_both(l, b):
        bzs[l, rows(b), :] = bown[l, rows(b), :].astype(BF16)
        bz_copy(l, b).start()
        bzso[l, rows(b), :] = bof[l, rows(b), :].astype(BF16)
        bz_other(l, b).start()

    def swap_sum(l, b):
        bys[l, rows(b), :] = bof[l, rows(b), :].astype(BF16)
        by_copy(l, b).start()

    def produce(l, carry):
        bof[l] = back(l, o)
        for k in one_down:
            swap_sum(l, blk(k))
        bown[l] = back(l, y)

        @pl.when(t == layers - 1)
        def _():
            for k in both_down:
                b = blk(k)

                @pl.when(l < t)
                def _():
                    send_both(l, b)

                @pl.when(l == t)
                def _():
                    swap_sum(l, b)

        return carry

    lax.fori_loop(0, t + 1, produce, 0)

    def collected(l, b):
        by_copy(l, b).wait_recv()
        return bown[l, rows(b), :] + byr[l, rows(b), :].astype(F32)

    def dec_piece(l):
        for h in range(2):
            piece = lax.dot_general(
                lat[l, h], og[...], (((0,), (0,)), ((), ())), preferred_element_type=F32
            )
            dec[l, h * half:(h + 1) * half, :] = piece.astype(BF16)
        dec_copy(l).start()

    def combine(l, carry):
        @pl.when(l < t)
        def _():
            @pl.when(t < layers - 1)
            def _():
                for k in both_down:
                    b = blk(k)
                    add_own(l, b)
                    add_other(l, b)
                    send_both(l, b)

            for k in one_down:
                b = blk(k)

                @pl.when(t < layers - 1)
                def _():
                    add_own(l, b)

                bzs[l, rows(b), :] = collected(l, b).astype(BF16)
                bz_copy(l, b).start()

        dec_piece(l)
        return carry

    lax.fori_loop(0, t + 1, combine, 0)

    def blank(l, carry):
        dec[l] = jnp.zeros((2 * half, dec.shape[2]), BF16)
        dec_copy(l).start()
        return carry

    lax.fori_loop(t + 1, layers, blank, 0)

    def final_copy(h, b):
        piece = pg.at[h, rows(b)]
        return rcopy(piece, piece, f_ss.at[b], f_rs.at[b], partner)

    @pl.when(t < layers - 1)
    def _():
        for k in both_down:
            b = blk(k)
            add_own(t, b)
            add_other(t, b)
            swap_sum(t, b)

    for k in one_down + both_down:
        b = blk(k)
        if k in one_down:
            @pl.when(t < layers - 1)
            def _():
                add_own(t, b)

        value = jnp.where(pre[rows(b), :] > 0.0, collected(t, b), 0.0)
        pg[y, rows(b), :] = value.astype(BF16)
        final_copy(y, b).start()
    for b in range(blocks):
        final_copy(o, b).wait_recv()
    own_dma = pltpu.make_async_copy(pg.at[y], pg_out.at[:, cols(y)], out_sem.at[1])
    other_dma = pltpu.make_async_copy(pg.at[o], pg_out.at[:, cols(o)], out_sem.at[2])
    own_dma.start()
    other_dma.start()

    for k in range(1, blocks):
        x_copy(k).wait_send()
    for c in range(chips):
        core_copy(c).wait_send()
        if c > 0:
            rs_copy(c).wait_send()
    for k in list(range(2, blocks, 2)) + [1]:
        og_copy(q, og_ss, k).wait_send()
    for k in range(2, blocks, 2):
        og_relay(k).wait_send()
    for b in range(blocks):
        part_copy(b).wait_send()
        final_copy(y, b).wait_send()

    def drain(l, carry):
        for k in range(blocks):
            b = blk(k)

            @pl.when(jnp.logical_or(l == t, k in one_up))
            def _():
                lat_swap(l, b).wait_send()

            @pl.when(jnp.logical_or(l == t, k in one_down))
            def _():
                by_copy(l, b).wait_send()

            @pl.when(t < layers - 1)
            def _():
                lat_up(l, b).wait_send()
                if k in both_up:
                    lat_up_other(l, b).wait_send()

            @pl.when(l < t)
            def _():
                bz_copy(l, b).wait_send()
                if k in both_down:
                    bz_other(l, b).wait_send()

        return carry

    lax.fori_loop(0, t + 1, drain, 0)
    for l in range(layers):
        dec_copy(l).wait()
    xg_copy.wait()
    own_dma.wait()
    other_dma.wait()


def exchange(layer_inputs, mlp_outputs, enc_weight, enc_bias, dec_weight):
    layers, latents, width = dec_weight.shape
    blocks = lax.axis_size("latent")
    rb, depth = layer_inputs.shape
    total_rows = rb * blocks
    half = latents // 2
    rscale = total_rows ** (-0.5)
    hbm = pl.BlockSpec(memory_space=pltpu.HBM)
    dma = pltpu.SemaphoreType.DMA
    per_block = dma((blocks,))
    per_layer = dma((layers, blocks))
    sums = pltpu.VMEM((layers, total_rows, half), F32)
    sent = pltpu.VMEM((layers, total_rows, half), BF16)
    one_half = pltpu.VMEM((total_rows, half), F32)
    row_blocks = pltpu.VMEM((blocks // 2, rb, width), BF16)
    per_chip = dma((blocks // 2,))
    return pl.pallas_call(
        functools.partial(exchange_kernel, layers, blocks, rscale),
        out_shape=(
            jax.ShapeDtypeStruct((layers, latents, width), BF16),
            jax.ShapeDtypeStruct((total_rows, depth), BF16),
            jax.ShapeDtypeStruct((total_rows, latents), BF16),
        ),
        in_specs=[hbm] * 5,
        out_specs=(pl.BlockSpec(memory_space=pl.ANY),) * 3,
        scratch_shapes=[
            pltpu.VMEM((total_rows, depth), BF16),
            pltpu.VMEM((rb, width), BF16),
            pltpu.VMEM((depth, latents), BF16),
            pltpu.VMEM((layers, latents), F32),
            pltpu.VMEM((layers, latents, width), BF16),
            one_half, one_half, one_half,
            pltpu.VMEM((layers, 2, total_rows, half), BF16),
            pltpu.VMEM((total_rows, width), F32),
            row_blocks, row_blocks, row_blocks, row_blocks,
            pltpu.VMEM((total_rows, width), BF16),
            sent, sent, sums, sums, sent, sent, sent, sent,
            pltpu.VMEM((2, total_rows, half), BF16),
            pltpu.VMEM((layers, latents, width), BF16),
            per_block, per_block, per_block, per_block,
            per_layer, per_layer, per_layer, per_layer, per_layer, per_layer,
            per_chip, per_chip, per_chip, per_chip, per_block, per_block, per_block,
            per_layer, per_layer, per_layer, per_layer, per_layer, per_layer,
            per_block, per_block,
            dma((5,)), dma((layers,)), dma((3,)),
        ],
        compiler_params=pltpu.CompilerParams(
            collective_id=0, has_side_effects=True, vmem_limit_bytes=56 * 2**20
        ),
        name="exchange",
    )(layer_inputs, mlp_outputs, enc_weight, enc_bias, dec_weight)


def local(layer_inputs, mlp_outputs, enc_weight, enc_bias, dec_weight):
    dec_grad, xg, pg = exchange(layer_inputs, mlp_outputs, enc_weight, enc_bias, dec_weight)
    enc_grad = lax.dot_general(xg, pg, (((0,), (0,)), ((), ())), preferred_element_type=F32)
    return (enc_grad, dec_grad)


def solution(mesh):
    in_specs = (
        P("latent", "layer"),
        P("latent", "layer"),
        P("layer", "latent"),
        P(None, "latent"),
        P(None, "latent", "layer"),
    )
    out_specs = (P("layer", "latent"), P(None, "latent", "layer"))
    return jax.shard_map(local, mesh=mesh, in_specs=in_specs, out_specs=out_specs, check_vma=False)
```

```python
import functools

import jax
import jax.numpy as jnp
from jax import lax
from jax.experimental import pallas as pl
from jax.experimental.pallas import tpu as pltpu
from jax.sharding import PartitionSpec as P

MESH = pl.DeviceIdType.MESH
F32 = jnp.float32
BF16 = jnp.bfloat16


def exchange_kernel(
    layers, blocks, rscale,
    x_hbm, mlp_hbm, w_hbm, bias_hbm, v_hbm,
    dec_out, xg_out, pg_out,
    xg, mlp, w, bias_all, v, part_send, part_recv, pre, lat, recon, core_send, core_recv, rs_send, rs_recv, og,
    bys, byr, bown, bof, bzs, bzr, bzso, bzro, pg, dec,
    x_ss, x_rs, p_ss, p_rs, z_ss, z_rs, zo_ss, zo_rs, y_ss, y_rs, core_ss, core_rs, rs_ss, rs_rs, og_ss, og_fs, og_rs,
    by_ss, by_rs, bz_ss, bz_rs, bzo_ss, bzo_rs, f_ss, f_rs, in_sem, dec_sem, out_sem,
):
    p = lax.axis_index("layer")
    q = lax.axis_index("latent")
    t = p // 2
    y = p % 2
    o = 1 - y
    rb = x_hbm.shape[0]
    half = w.shape[1] // 2
    partner = (p + 1 - 2 * y, q)
    up = (p + 2, q)
    down = (p - 2, q)
    chips = blocks // 2

    def blk(k):
        return ((q // 2 + k // 2) % chips) * 2 + (q % 2 + k % 2) % 2

    def rows(b):
        return pl.ds(pl.multiple_of(b * rb, rb), rb)

    def cols(h):
        return pl.ds(pl.multiple_of(h * half, half), half)

    def rcopy(src, dst, ss, rs, dev):
        return pltpu.make_async_remote_copy(
            src_ref=src, dst_ref=dst, send_sem=ss, recv_sem=rs, device_id=dev, device_id_type=MESH
        )

    own_x = pltpu.make_async_copy(x_hbm, xg.at[rows(q)], in_sem.at[0])
    w_copy = pltpu.make_async_copy(w_hbm, w, in_sem.at[1])
    bias_copy = pltpu.make_async_copy(bias_hbm, bias_all, in_sem.at[2])
    mlp_copy = pltpu.make_async_copy(mlp_hbm, mlp, in_sem.at[3])
    v_copy = pltpu.make_async_copy(v_hbm, v, in_sem.at[4])
    for copy in (own_x, w_copy, bias_copy, mlp_copy, v_copy):
        copy.start()
    both_up = list(range(blocks // 2, blocks))
    one_up = list(range(blocks // 2))
    both_down = list(range(blocks - max(blocks // 4, 1), blocks))
    one_down = list(range(blocks - max(blocks // 4, 1)))

    barrier = pltpu.get_barrier_semaphore()
    for k in range(1, blocks):
        pl.semaphore_signal(barrier, inc=1, device_id=(p, blk(k)), device_id_type=MESH)
    pl.semaphore_signal(barrier, inc=1, device_id=partner, device_id_type=MESH)

    @pl.when(t < layers - 1)
    def _():
        pl.semaphore_signal(barrier, inc=1, device_id=up, device_id_type=MESH)

    @pl.when(t > 0)
    def _():
        pl.semaphore_signal(barrier, inc=1, device_id=down, device_id_type=MESH)

    neighbours = blocks + (t < layers - 1).astype(jnp.int32) + (t > 0).astype(jnp.int32)
    pl.semaphore_wait(barrier, neighbours)

    def x_copy(k):
        return rcopy(x_hbm, xg.at[rows(q)], x_ss.at[k], x_rs.at[q], (p, blk(k)))

    for k in list(range(2, blocks)) + [1]:
        x_copy(k).start()

    def part_copy(b):
        return rcopy(part_send.at[rows(b)], part_recv.at[rows(b)], p_ss.at[b], p_rs.at[b], partner)

    def lat_up(l, b):
        piece = lat.at[l, y, rows(b)]
        return rcopy(piece, piece, z_ss.at[l, b], z_rs.at[l, b], up)

    def lat_up_other(l, b):
        piece = lat.at[l, o, rows(b)]
        return rcopy(piece, piece, zo_ss.at[l, b], zo_rs.at[l, b], up)

    def lat_swap(l, b):
        piece = lat.at[l, y, rows(b)]
        return rcopy(piece, piece, y_ss.at[l, b], y_rs.at[l, b], partner)

    def lat_swap_in(l, b):
        piece = lat.at[l, o, rows(b)]
        return rcopy(piece, piece, y_ss.at[l, b], y_rs.at[l, b], partner)

    def own_block(b):
        part_copy(b).wait_recv()
        total = pre[rows(b), :] + part_recv[rows(b), :] + bias
        pre[rows(b), :] = total
        lat[t, y, rows(b), :] = jnp.maximum(total, 0.0).astype(BF16)

        @pl.when(t < layers - 1)
        def _():
            lat_up(t, b).start()

        lat_swap(t, b).start()

    def relay(l, k):
        b = blk(k)
        lat_up(l, b).wait_recv()

        @pl.when(t < layers - 1)
        def _():
            lat_up(l, b).start()

        if k in one_up:
            lat_swap(l, b).start()

    def relay_below(k):
        @pl.when(t > 0)
        def _():
            relay(t - 1, k)

    bias_copy.wait()
    bias_half = jnp.where(y == 0, bias_all[:, :half], bias_all[:, half:])
    own_row = lax.broadcasted_iota(jnp.int32, bias_half.shape, 0) == t
    bias = jnp.sum(jnp.where(own_row, bias_half, 0.0), axis=0, keepdims=True)
    own_x.wait()
    w_copy.wait()
    for k in range(blocks):
        b = blk(k)
        if k > 0:
            rcopy(x_hbm, xg.at[rows(b)], x_ss.at[k], x_rs.at[b], (p, b)).wait_recv()
        part_send[rows(b), :] = jnp.dot(xg[rows(b), :], w[:, cols(o)], preferred_element_type=F32)
        part_copy(b).start()
        pre[rows(b), :] = jnp.dot(xg[rows(b), :], w[:, cols(y)], preferred_element_type=F32)
        if k > 0:
            own_block(blk(k - 1))
        if k > 1:
            relay_below(k - 2)
    own_block(blk(blocks - 1))
    relay_below(blocks - 2)
    relay_below(blocks - 1)
    xg_copy = pltpu.make_async_copy(xg, xg_out, out_sem.at[0])
    xg_copy.start()

    recon[...] = jnp.zeros_like(recon)
    v_copy.wait()

    def decode(l, h):
        recon[...] += jnp.dot(lat[l, h], v[l, cols(h), :], preferred_element_type=F32)

    def other_up(l, b):
        @pl.when(t < layers - 1)
        def _():
            lat_up_other(l, b).start()

    def forward(s, carry):
        l = t - s

        @pl.when(jnp.logical_and(s > 1, s <= t))
        def _():
            for k in range(blocks):
                relay(l, k)

        @pl.when(s <= t)
        def _():
            decode(l, y)

        @pl.when(s > 0)
        def _():
            for k in both_up:
                b = blk(k)

                @pl.when(s == 1)
                def _():
                    lat_swap_in(t, b).wait_recv()

                @pl.when(s > 1)
                def _():
                    lat_up_other(l + 1, b).wait_recv()

                other_up(l + 1, b)
            for k in one_up:
                lat_swap_in(l + 1, blk(k)).wait_recv()
            decode(l + 1, o)

        return carry

    lax.fori_loop(0, t + 2, forward, 0)

    def core_copy(c):
        return rcopy(core_send.at[c], core_recv.at[c], core_ss.at[c], core_rs.at[c], (p, blk(1)))

    def rs_copy(c):
        return rcopy(rs_send.at[c], rs_recv.at[q // 2], rs_ss.at[c], rs_rs.at[q // 2], (p, blk(2 * c)))

    def rs_in(c):
        chip = (q // 2 + c) % chips
        return rcopy(rs_send.at[c], rs_recv.at[chip], rs_ss.at[c], rs_rs.at[chip], (p, blk(2 * c)))

    order = list(range(1, chips)) + [0]
    for c in order:
        core_send[c] = recon[rows(blk(2 * c + 1)), :].astype(BF16)
        core_copy(c).start()
    for c in order:
        core_copy(c).wait_recv()
        total = recon[rows(blk(2 * c)), :] + core_recv[c].astype(F32)
        if c > 0:
            rs_send[c] = total.astype(BF16)
            rs_copy(c).start()
    mlp_copy.wait()
    for c in range(1, chips):
        rs_in(c).wait_recv()
        total = total + rs_recv[(q // 2 + c) % chips].astype(F32)
    og[rows(q), :] = ((total - mlp[...].astype(F32)) * rscale).astype(BF16)

    def og_copy(src, ss, k):
        return rcopy(og.at[rows(src)], og.at[rows(src)], ss.at[k], og_rs.at[src], (p, blk(k)))

    def og_relay(k):
        return rcopy(og.at[rows(blk(k))], og.at[rows(blk(k))], og_fs.at[k], og_rs.at[blk(k)], (p, blk(1)))

    for k in list(range(2, blocks, 2)) + [1]:
        og_copy(q, og_ss, k).start()
    for k in range(2, blocks, 2):
        og_copy(blk(k), og_ss, k).wait_recv()
        og_relay(k).start()
    for k in range(1, blocks, 2):
        og_copy(blk(k), og_ss, k).wait_recv()

    def by_copy(l, b):
        return rcopy(bys.at[l, rows(b)], byr.at[l, rows(b)], by_ss.at[l, b], by_rs.at[l, b], partner)

    def bz_copy(l, b):
        return rcopy(bzs.at[l, rows(b)], bzr.at[l, rows(b)], bz_ss.at[l, b], bz_rs.at[l, b], down)

    def bz_other(l, b):
        return rcopy(bzso.at[l, rows(b)], bzro.at[l, rows(b)], bzo_ss.at[l, b], bzo_rs.at[l, b], down)

    def dec_copy(l):
        return pltpu.make_async_copy(dec.at[l], dec_out.at[l], dec_sem.at[l])

    def back(l, h):
        return lax.dot_general(
            og[...], v[l, cols(h), :], (((1,), (1,)), ((), ())), preferred_element_type=F32
        )

    def add_own(l, b):
        bz_copy(l, b).wait_recv()
        bown[l, rows(b), :] += bzr[l, rows(b), :].astype(F32)

    def add_other(l, b):
        bz_other(l, b).wait_recv()
        bof[l, rows(b), :] += bzro[l, rows(b), :].astype(F32)

    def send_both(l, b):
        bzs[l, rows(b), :] = bown[l, rows(b), :].astype(BF16)
        bz_copy(l, b).start()
        bzso[l, rows(b), :] = bof[l, rows(b), :].astype(BF16)
        bz_other(l, b).start()

    def swap_sum(l, b):
        bys[l, rows(b), :] = bof[l, rows(b), :].astype(BF16)
        by_copy(l, b).start()

    def produce(l, carry):
        bof[l] = back(l, o)
        for k in one_down:
            swap_sum(l, blk(k))
        bown[l] = back(l, y)

        @pl.when(t == layers - 1)
        def _():
            for k in both_down:
                b = blk(k)

                @pl.when(l < t)
                def _():
                    send_both(l, b)

                @pl.when(l == t)
                def _():
                    swap_sum(l, b)

        return carry

    lax.fori_loop(0, t + 1, produce, 0)

    def collected(l, b):
        by_copy(l, b).wait_recv()
        return bown[l, rows(b), :] + byr[l, rows(b), :].astype(F32)

    def dec_piece(l):
        for h in range(2):
            piece = lax.dot_general(
                lat[l, h], og[...], (((0,), (0,)), ((), ())), preferred_element_type=F32
            )
            dec[l, h * half:(h + 1) * half, :] = piece.astype(BF16)
        dec_copy(l).start()

    def combine_both(l, carry):
        for k in both_down:
            b = blk(k)
            add_own(l, b)
            add_other(l, b)

            @pl.when(l < t)
            def _():
                send_both(l, b)

            @pl.when(l == t)
            def _():
                swap_sum(l, b)

        return carry

    @pl.when(t < layers - 1)
    def _():
        lax.fori_loop(0, t + 1, combine_both, 0)

    def combine(l, carry):
        @pl.when(l < t)
        def _():
            for k in one_down:
                b = blk(k)

                @pl.when(t < layers - 1)
                def _():
                    add_own(l, b)

                bzs[l, rows(b), :] = collected(l, b).astype(BF16)
                bz_copy(l, b).start()

        dec_piece(l)
        return carry

    lax.fori_loop(0, t + 1, combine, 0)

    def blank(l, carry):
        dec[l] = jnp.zeros((2 * half, dec.shape[2]), BF16)
        dec_copy(l).start()
        return carry

    lax.fori_loop(t + 1, layers, blank, 0)

    def final_copy(h, b):
        piece = pg.at[h, rows(b)]
        return rcopy(piece, piece, f_ss.at[b], f_rs.at[b], partner)

    for k in both_down + one_down:
        b = blk(k)
        if k in one_down:
            @pl.when(t < layers - 1)
            def _():
                add_own(t, b)

        value = jnp.where(pre[rows(b), :] > 0.0, collected(t, b), 0.0)
        pg[y, rows(b), :] = value.astype(BF16)
        final_copy(y, b).start()
    for b in range(blocks):
        final_copy(o, b).wait_recv()
    own_dma = pltpu.make_async_copy(pg.at[y], pg_out.at[:, cols(y)], out_sem.at[1])
    other_dma = pltpu.make_async_copy(pg.at[o], pg_out.at[:, cols(o)], out_sem.at[2])
    own_dma.start()
    other_dma.start()

    for k in range(1, blocks):
        x_copy(k).wait_send()
    for c in range(chips):
        core_copy(c).wait_send()
        if c > 0:
            rs_copy(c).wait_send()
    for k in list(range(2, blocks, 2)) + [1]:
        og_copy(q, og_ss, k).wait_send()
    for k in range(2, blocks, 2):
        og_relay(k).wait_send()
    for b in range(blocks):
        part_copy(b).wait_send()
        final_copy(y, b).wait_send()

    def drain(l, carry):
        for k in range(blocks):
            b = blk(k)

            @pl.when(jnp.logical_or(l == t, k in one_up))
            def _():
                lat_swap(l, b).wait_send()

            @pl.when(jnp.logical_or(l == t, k in one_down))
            def _():
                by_copy(l, b).wait_send()

            @pl.when(t < layers - 1)
            def _():
                lat_up(l, b).wait_send()
                if k in both_up:
                    lat_up_other(l, b).wait_send()

            @pl.when(l < t)
            def _():
                bz_copy(l, b).wait_send()
                if k in both_down:
                    bz_other(l, b).wait_send()

        return carry

    lax.fori_loop(0, t + 1, drain, 0)
    for l in range(layers):
        dec_copy(l).wait()
    xg_copy.wait()
    own_dma.wait()
    other_dma.wait()


def exchange(layer_inputs, mlp_outputs, enc_weight, enc_bias, dec_weight):
    layers, latents, width = dec_weight.shape
    blocks = lax.axis_size("latent")
    rb, depth = layer_inputs.shape
    total_rows = rb * blocks
    half = latents // 2
    rscale = total_rows ** (-0.5)
    hbm = pl.BlockSpec(memory_space=pltpu.HBM)
    dma = pltpu.SemaphoreType.DMA
    per_block = dma((blocks,))
    per_layer = dma((layers, blocks))
    sums = pltpu.VMEM((layers, total_rows, half), F32)
    sent = pltpu.VMEM((layers, total_rows, half), BF16)
    one_half = pltpu.VMEM((total_rows, half), F32)
    row_blocks = pltpu.VMEM((blocks // 2, rb, width), BF16)
    per_chip = dma((blocks // 2,))
    return pl.pallas_call(
        functools.partial(exchange_kernel, layers, blocks, rscale),
        out_shape=(
            jax.ShapeDtypeStruct((layers, latents, width), BF16),
            jax.ShapeDtypeStruct((total_rows, depth), BF16),
            jax.ShapeDtypeStruct((total_rows, latents), BF16),
        ),
        in_specs=[hbm] * 5,
        out_specs=(pl.BlockSpec(memory_space=pl.ANY),) * 3,
        scratch_shapes=[
            pltpu.VMEM((total_rows, depth), BF16),
            pltpu.VMEM((rb, width), BF16),
            pltpu.VMEM((depth, latents), BF16),
            pltpu.VMEM((layers, latents), F32),
            pltpu.VMEM((layers, latents, width), BF16),
            one_half, one_half, one_half,
            pltpu.VMEM((layers, 2, total_rows, half), BF16),
            pltpu.VMEM((total_rows, width), F32),
            row_blocks, row_blocks, row_blocks, row_blocks,
            pltpu.VMEM((total_rows, width), BF16),
            sent, sent, sums, sums, sent, sent, sent, sent,
            pltpu.VMEM((2, total_rows, half), BF16),
            pltpu.VMEM((layers, latents, width), BF16),
            per_block, per_block, per_block, per_block,
            per_layer, per_layer, per_layer, per_layer, per_layer, per_layer,
            per_chip, per_chip, per_chip, per_chip, per_block, per_block, per_block,
            per_layer, per_layer, per_layer, per_layer, per_layer, per_layer,
            per_block, per_block,
            dma((5,)), dma((layers,)), dma((3,)),
        ],
        compiler_params=pltpu.CompilerParams(
            collective_id=0, has_side_effects=True, vmem_limit_bytes=56 * 2**20
        ),
        name="exchange",
    )(layer_inputs, mlp_outputs, enc_weight, enc_bias, dec_weight)


def local(layer_inputs, mlp_outputs, enc_weight, enc_bias, dec_weight):
    dec_grad, xg, pg = exchange(layer_inputs, mlp_outputs, enc_weight, enc_bias, dec_weight)
    enc_grad = lax.dot_general(xg, pg, (((0,), (0,)), ((), ())), preferred_element_type=F32)
    return (enc_grad, dec_grad)


def solution(mesh):
    in_specs = (
        P("latent", "layer"),
        P("latent", "layer"),
        P("layer", "latent"),
        P(None, "latent"),
        P(None, "latent", "layer"),
    )
    out_specs = (P("layer", "latent"), P(None, "latent", "layer"))
    return jax.shard_map(local, mesh=mesh, in_specs=in_specs, out_specs=out_specs, check_vma=False)
```

```python
import functools

import jax
import jax.numpy as jnp
from jax import lax
from jax.experimental import pallas as pl
from jax.experimental.pallas import tpu as pltpu
from jax.sharding import PartitionSpec as P

MESH = pl.DeviceIdType.MESH
F32 = jnp.float32
BF16 = jnp.bfloat16


def exchange_kernel(
    layers, blocks, rscale,
    x_hbm, mlp_hbm, w_hbm, bias_hbm, v_hbm,
    dec_out, xg_out, pg_out,
    xg, mlp, w, bias_all, v, part_send, part_recv, pre, lat, recon, core_send, core_recv, rs_send, rs_recv, og,
    bys, byr, bown, bof, bzs, bzr, bzso, bzro, pg, dec,
    x_ss, x_rs, p_ss, p_rs, z_ss, z_rs, zo_ss, zo_rs, y_ss, y_rs, core_ss, core_rs, rs_ss, rs_rs, og_ss, og_fs, og_rs,
    by_ss, by_rs, bz_ss, bz_rs, bzo_ss, bzo_rs, f_ss, f_rs, in_sem, dec_sem, out_sem,
):
    p = lax.axis_index("layer")
    q = lax.axis_index("latent")
    t = p // 2
    y = p % 2
    o = 1 - y
    rb = x_hbm.shape[0]
    half = w.shape[1] // 2
    partner = (p + 1 - 2 * y, q)
    up = (p + 2, q)
    down = (p - 2, q)
    chips = blocks // 2

    def blk(k):
        return ((q // 2 + k // 2) % chips) * 2 + (q % 2 + k % 2) % 2

    def rows(b):
        return pl.ds(pl.multiple_of(b * rb, rb), rb)

    def cols(h):
        return pl.ds(pl.multiple_of(h * half, half), half)

    def rcopy(src, dst, ss, rs, dev):
        return pltpu.make_async_remote_copy(
            src_ref=src, dst_ref=dst, send_sem=ss, recv_sem=rs, device_id=dev, device_id_type=MESH
        )

    own_x = pltpu.make_async_copy(x_hbm, xg.at[rows(q)], in_sem.at[0])
    w_copy = pltpu.make_async_copy(w_hbm, w, in_sem.at[1])
    bias_copy = pltpu.make_async_copy(bias_hbm, bias_all, in_sem.at[2])
    mlp_copy = pltpu.make_async_copy(mlp_hbm, mlp, in_sem.at[3])
    v_copy = pltpu.make_async_copy(v_hbm, v, in_sem.at[4])
    for copy in (own_x, w_copy, bias_copy, mlp_copy, v_copy):
        copy.start()
    both_up = list(range(blocks // 2, blocks))
    one_up = list(range(blocks // 2))
    both_down = list(range(blocks - max(blocks // 4, 1), blocks))
    one_down = list(range(blocks - max(blocks // 4, 1)))

    barrier = pltpu.get_barrier_semaphore()
    for k in range(1, blocks):
        pl.semaphore_signal(barrier, inc=1, device_id=(p, blk(k)), device_id_type=MESH)
    pl.semaphore_signal(barrier, inc=1, device_id=partner, device_id_type=MESH)

    @pl.when(t < layers - 1)
    def _():
        pl.semaphore_signal(barrier, inc=1, device_id=up, device_id_type=MESH)

    @pl.when(t > 0)
    def _():
        pl.semaphore_signal(barrier, inc=1, device_id=down, device_id_type=MESH)

    neighbours = blocks + (t < layers - 1).astype(jnp.int32) + (t > 0).astype(jnp.int32)
    pl.semaphore_wait(barrier, neighbours)

    def x_copy(k):
        return rcopy(x_hbm, xg.at[rows(q)], x_ss.at[k], x_rs.at[q], (p, blk(k)))

    for k in list(range(2, blocks)) + [1]:
        x_copy(k).start()

    def part_copy(b):
        return rcopy(part_send.at[rows(b)], part_recv.at[rows(b)], p_ss.at[b], p_rs.at[b], partner)

    def lat_up(l, b):
        piece = lat.at[l, y, rows(b)]
        return rcopy(piece, piece, z_ss.at[l, b], z_rs.at[l, b], up)

    def lat_up_other(l, b):
        piece = lat.at[l, o, rows(b)]
        return rcopy(piece, piece, zo_ss.at[l, b], zo_rs.at[l, b], up)

    def lat_swap(l, b):
        piece = lat.at[l, y, rows(b)]
        return rcopy(piece, piece, y_ss.at[l, b], y_rs.at[l, b], partner)

    def lat_swap_in(l, b):
        piece = lat.at[l, o, rows(b)]
        return rcopy(piece, piece, y_ss.at[l, b], y_rs.at[l, b], partner)

    def own_block(b):
        part_copy(b).wait_recv()
        total = pre[rows(b), :] + part_recv[rows(b), :] + bias
        pre[rows(b), :] = total
        lat[t, y, rows(b), :] = jnp.maximum(total, 0.0).astype(BF16)

        @pl.when(t < layers - 1)
        def _():
            lat_up(t, b).start()

        lat_swap(t, b).start()

    def relay(l, k):
        b = blk(k)
        lat_up(l, b).wait_recv()

        @pl.when(t < layers - 1)
        def _():
            lat_up(l, b).start()

        if k in one_up:
            lat_swap(l, b).start()

    def relay_below(k):
        @pl.when(t > 0)
        def _():
            relay(t - 1, k)

    bias_copy.wait()
    bias_half = jnp.where(y == 0, bias_all[:, :half], bias_all[:, half:])
    own_row = lax.broadcasted_iota(jnp.int32, bias_half.shape, 0) == t
    bias = jnp.sum(jnp.where(own_row, bias_half, 0.0), axis=0, keepdims=True)
    own_x.wait()
    w_copy.wait()
    for k in range(blocks):
        b = blk(k)
        if k > 0:
            rcopy(x_hbm, xg.at[rows(b)], x_ss.at[k], x_rs.at[b], (p, b)).wait_recv()
        part_send[rows(b), :] = jnp.dot(xg[rows(b), :], w[:, cols(o)], preferred_element_type=F32)
        part_copy(b).start()
        pre[rows(b), :] = jnp.dot(xg[rows(b), :], w[:, cols(y)], preferred_element_type=F32)
        if k > 0:
            own_block(blk(k - 1))
        if k > 1:
            relay_below(k - 2)
    own_block(blk(blocks - 1))
    relay_below(blocks - 2)
    relay_below(blocks - 1)
    xg_copy = pltpu.make_async_copy(xg, xg_out, out_sem.at[0])
    xg_copy.start()

    recon[...] = jnp.zeros_like(recon)
    v_copy.wait()

    def decode(l, h):
        recon[...] += jnp.dot(lat[l, h], v[l, cols(h), :], preferred_element_type=F32)

    def other_up(l, b):
        @pl.when(t < layers - 1)
        def _():
            lat_up_other(l, b).start()

    def forward(s, carry):
        l = t - s

        @pl.when(jnp.logical_and(s > 1, s <= t))
        def _():
            for k in range(blocks):
                relay(l, k)

        @pl.when(s <= t)
        def _():
            decode(l, y)

        @pl.when(s > 0)
        def _():
            for k in both_up:
                b = blk(k)

                @pl.when(s == 1)
                def _():
                    lat_swap_in(t, b).wait_recv()

                @pl.when(s > 1)
                def _():
                    lat_up_other(l + 1, b).wait_recv()

                other_up(l + 1, b)
            for k in one_up:
                lat_swap_in(l + 1, blk(k)).wait_recv()
            decode(l + 1, o)

        return carry

    lax.fori_loop(0, t + 2, forward, 0)

    def core_copy(c):
        return rcopy(core_send.at[c], core_recv.at[c], core_ss.at[c], core_rs.at[c], (p, blk(1)))

    def rs_copy(c):
        return rcopy(rs_send.at[c], rs_recv.at[q // 2], rs_ss.at[c], rs_rs.at[q // 2], (p, blk(2 * c)))

    def rs_in(c):
        chip = (q // 2 + c) % chips
        return rcopy(rs_send.at[c], rs_recv.at[chip], rs_ss.at[c], rs_rs.at[chip], (p, blk(2 * c)))

    order = list(range(1, chips)) + [0]
    for c in order:
        core_send[c] = recon[rows(blk(2 * c + 1)), :].astype(BF16)
        core_copy(c).start()
    for c in order:
        core_copy(c).wait_recv()
        total = recon[rows(blk(2 * c)), :] + core_recv[c].astype(F32)
        if c > 0:
            rs_send[c] = total.astype(BF16)
            rs_copy(c).start()
    mlp_copy.wait()
    for c in range(1, chips):
        rs_in(c).wait_recv()
        total = total + rs_recv[(q // 2 + c) % chips].astype(F32)
    og[rows(q), :] = ((total - mlp[...].astype(F32)) * rscale).astype(BF16)

    def og_copy(src, ss, k):
        return rcopy(og.at[rows(src)], og.at[rows(src)], ss.at[k], og_rs.at[src], (p, blk(k)))

    def og_relay(k):
        return rcopy(og.at[rows(blk(k))], og.at[rows(blk(k))], og_fs.at[k], og_rs.at[blk(k)], (p, blk(1)))

    for k in list(range(2, blocks, 2)) + [1]:
        og_copy(q, og_ss, k).start()
    for k in range(2, blocks, 2):
        og_copy(blk(k), og_ss, k).wait_recv()
        og_relay(k).start()
    for k in range(1, blocks, 2):
        og_copy(blk(k), og_ss, k).wait_recv()

    def by_copy(l, b):
        return rcopy(bys.at[l, rows(b)], byr.at[l, rows(b)], by_ss.at[l, b], by_rs.at[l, b], partner)

    def bz_copy(l, b):
        return rcopy(bzs.at[l, rows(b)], bzr.at[l, rows(b)], bz_ss.at[l, b], bz_rs.at[l, b], down)

    def bz_other(l, b):
        return rcopy(bzso.at[l, rows(b)], bzro.at[l, rows(b)], bzo_ss.at[l, b], bzo_rs.at[l, b], down)

    def dec_copy(l):
        return pltpu.make_async_copy(dec.at[l], dec_out.at[l], dec_sem.at[l])

    def back(l, h):
        return lax.dot_general(
            og[...], v[l, cols(h), :], (((1,), (1,)), ((), ())), preferred_element_type=F32
        )

    def add_own(l, b):
        bz_copy(l, b).wait_recv()
        bown[l, rows(b), :] += bzr[l, rows(b), :].astype(F32)

    def add_other(l, b):
        bz_other(l, b).wait_recv()
        bof[l, rows(b), :] += bzro[l, rows(b), :].astype(F32)

    def send_both(l, b):
        bzs[l, rows(b), :] = bown[l, rows(b), :].astype(BF16)
        bz_copy(l, b).start()
        bzso[l, rows(b), :] = bof[l, rows(b), :].astype(BF16)
        bz_other(l, b).start()

    def swap_sum(l, b):
        bys[l, rows(b), :] = bof[l, rows(b), :].astype(BF16)
        by_copy(l, b).start()

    def produce(l, carry):
        bof[l] = back(l, o)

        @pl.when(jnp.logical_and(t == layers - 1, l == t))
        def _():
            for k in both_down:
                swap_sum(l, blk(k))

        for k in one_down:
            swap_sum(l, blk(k))
        bown[l] = back(l, y)

        @pl.when(t == layers - 1)
        def _():
            for k in both_down:
                b = blk(k)

                @pl.when(l < t)
                def _():
                    send_both(l, b)

        return carry

    lax.fori_loop(0, t + 1, produce, 0)

    def collected(l, b):
        by_copy(l, b).wait_recv()
        return bown[l, rows(b), :] + byr[l, rows(b), :].astype(F32)

    def dec_piece(l):
        for h in range(2):
            piece = lax.dot_general(
                lat[l, h], og[...], (((0,), (0,)), ((), ())), preferred_element_type=F32
            )
            dec[l, h * half:(h + 1) * half, :] = piece.astype(BF16)
        dec_copy(l).start()

    def combine_both(l, carry):
        for k in both_down:
            b = blk(k)
            add_own(l, b)
            add_other(l, b)

            @pl.when(l < t)
            def _():
                send_both(l, b)

            @pl.when(l == t)
            def _():
                swap_sum(l, b)

        return carry

    @pl.when(t < layers - 1)
    def _():
        lax.fori_loop(0, t + 1, combine_both, 0)

    def combine(l, carry):
        @pl.when(l < t)
        def _():
            for k in one_down:
                b = blk(k)

                @pl.when(t < layers - 1)
                def _():
                    add_own(l, b)

                bzs[l, rows(b), :] = collected(l, b).astype(BF16)
                bz_copy(l, b).start()

        dec_piece(l)
        return carry

    lax.fori_loop(0, t + 1, combine, 0)

    def blank(l, carry):
        dec[l] = jnp.zeros((2 * half, dec.shape[2]), BF16)
        dec_copy(l).start()
        return carry

    lax.fori_loop(t + 1, layers, blank, 0)

    def final_copy(h, b):
        piece = pg.at[h, rows(b)]
        return rcopy(piece, piece, f_ss.at[b], f_rs.at[b], partner)

    for k in both_down + one_down:
        b = blk(k)
        if k in one_down:
            @pl.when(t < layers - 1)
            def _():
                add_own(t, b)

        value = jnp.where(pre[rows(b), :] > 0.0, collected(t, b), 0.0)
        pg[y, rows(b), :] = value.astype(BF16)
        final_copy(y, b).start()
    for b in range(blocks):
        final_copy(o, b).wait_recv()
    own_dma = pltpu.make_async_copy(pg.at[y], pg_out.at[:, cols(y)], out_sem.at[1])
    other_dma = pltpu.make_async_copy(pg.at[o], pg_out.at[:, cols(o)], out_sem.at[2])
    own_dma.start()
    other_dma.start()

    for k in range(1, blocks):
        x_copy(k).wait_send()
    for c in range(chips):
        core_copy(c).wait_send()
        if c > 0:
            rs_copy(c).wait_send()
    for k in list(range(2, blocks, 2)) + [1]:
        og_copy(q, og_ss, k).wait_send()
    for k in range(2, blocks, 2):
        og_relay(k).wait_send()
    for b in range(blocks):
        part_copy(b).wait_send()
        final_copy(y, b).wait_send()

    def drain(l, carry):
        for k in range(blocks):
            b = blk(k)

            @pl.when(jnp.logical_or(l == t, k in one_up))
            def _():
                lat_swap(l, b).wait_send()

            @pl.when(jnp.logical_or(l == t, k in one_down))
            def _():
                by_copy(l, b).wait_send()

            @pl.when(t < layers - 1)
            def _():
                lat_up(l, b).wait_send()
                if k in both_up:
                    lat_up_other(l, b).wait_send()

            @pl.when(l < t)
            def _():
                bz_copy(l, b).wait_send()
                if k in both_down:
                    bz_other(l, b).wait_send()

        return carry

    lax.fori_loop(0, t + 1, drain, 0)
    for l in range(layers):
        dec_copy(l).wait()
    xg_copy.wait()
    own_dma.wait()
    other_dma.wait()


def exchange(layer_inputs, mlp_outputs, enc_weight, enc_bias, dec_weight):
    layers, latents, width = dec_weight.shape
    blocks = lax.axis_size("latent")
    rb, depth = layer_inputs.shape
    total_rows = rb * blocks
    half = latents // 2
    rscale = total_rows ** (-0.5)
    hbm = pl.BlockSpec(memory_space=pltpu.HBM)
    dma = pltpu.SemaphoreType.DMA
    per_block = dma((blocks,))
    per_layer = dma((layers, blocks))
    sums = pltpu.VMEM((layers, total_rows, half), F32)
    sent = pltpu.VMEM((layers, total_rows, half), BF16)
    one_half = pltpu.VMEM((total_rows, half), F32)
    row_blocks = pltpu.VMEM((blocks // 2, rb, width), BF16)
    per_chip = dma((blocks // 2,))
    return pl.pallas_call(
        functools.partial(exchange_kernel, layers, blocks, rscale),
        out_shape=(
            jax.ShapeDtypeStruct((layers, latents, width), BF16),
            jax.ShapeDtypeStruct((total_rows, depth), BF16),
            jax.ShapeDtypeStruct((total_rows, latents), BF16),
        ),
        in_specs=[hbm] * 5,
        out_specs=(pl.BlockSpec(memory_space=pl.ANY),) * 3,
        scratch_shapes=[
            pltpu.VMEM((total_rows, depth), BF16),
            pltpu.VMEM((rb, width), BF16),
            pltpu.VMEM((depth, latents), BF16),
            pltpu.VMEM((layers, latents), F32),
            pltpu.VMEM((layers, latents, width), BF16),
            one_half, one_half, one_half,
            pltpu.VMEM((layers, 2, total_rows, half), BF16),
            pltpu.VMEM((total_rows, width), F32),
            row_blocks, row_blocks, row_blocks, row_blocks,
            pltpu.VMEM((total_rows, width), BF16),
            sent, sent, sums, sums, sent, sent, sent, sent,
            pltpu.VMEM((2, total_rows, half), BF16),
            pltpu.VMEM((layers, latents, width), BF16),
            per_block, per_block, per_block, per_block,
            per_layer, per_layer, per_layer, per_layer, per_layer, per_layer,
            per_chip, per_chip, per_chip, per_chip, per_block, per_block, per_block,
            per_layer, per_layer, per_layer, per_layer, per_layer, per_layer,
            per_block, per_block,
            dma((5,)), dma((layers,)), dma((3,)),
        ],
        compiler_params=pltpu.CompilerParams(
            collective_id=0, has_side_effects=True, vmem_limit_bytes=56 * 2**20
        ),
        name="exchange",
    )(layer_inputs, mlp_outputs, enc_weight, enc_bias, dec_weight)


def finish_kernel(
    xg_hbm, pg_hbm, dec_hbm, enc_out, dec_out, xg, pg, enc, dec, in_sem, dec_in, dec_sem, enc_sem
):
    layers = dec.shape[0]
    piece = enc.shape[0] // layers
    ins = [
        pltpu.make_async_copy(xg_hbm, xg, in_sem.at[0]),
        pltpu.make_async_copy(pg_hbm, pg, in_sem.at[1]),
    ]
    reads = [pltpu.make_async_copy(dec_hbm.at[l], dec.at[l], dec_in.at[l]) for l in range(layers)]
    for copy in ins + reads:
        copy.start()
    for copy in ins:
        copy.wait()
    writes = []
    for l in range(layers):
        part = pl.ds(l * piece, piece)
        enc[part, :] = lax.dot_general(
            xg[:, part], pg[...], (((0,), (0,)), ((), ())), preferred_element_type=F32
        )
        writes.append(pltpu.make_async_copy(enc.at[part], enc_out.at[part], enc_sem.at[l]))
        writes[-1].start()
        reads[l].wait()
        writes.append(pltpu.make_async_copy(dec.at[l], dec_out.at[l], dec_sem.at[l]))
        writes[-1].start()
    for copy in writes:
        copy.wait()


def local(layer_inputs, mlp_outputs, enc_weight, enc_bias, dec_weight):
    dec, xg, pg = exchange(layer_inputs, mlp_outputs, enc_weight, enc_bias, dec_weight)
    hbm = pl.BlockSpec(memory_space=pltpu.HBM)
    per_layer = pltpu.SemaphoreType.DMA((dec.shape[0],))
    return pl.pallas_call(
        finish_kernel,
        in_specs=[hbm] * 3,
        out_specs=(hbm,) * 2,
        out_shape=(
            jax.ShapeDtypeStruct(enc_weight.shape, F32),
            jax.ShapeDtypeStruct(dec_weight.shape, BF16),
        ),
        scratch_shapes=[
            pltpu.VMEM(xg.shape, BF16),
            pltpu.VMEM(pg.shape, BF16),
            pltpu.VMEM(enc_weight.shape, F32),
            pltpu.VMEM(dec.shape, BF16),
            pltpu.SemaphoreType.DMA((2,)),
            per_layer, per_layer, per_layer,
        ],
        compiler_params=pltpu.CompilerParams(vmem_limit_bytes=56 * 2**20),
        name="finish",
    )(xg, pg, dec)


def solution(mesh):
    in_specs = (
        P("latent", "layer"),
        P("latent", "layer"),
        P("layer", "latent"),
        P(None, "latent"),
        P(None, "latent", "layer"),
    )
    out_specs = (P("layer", "latent"), P(None, "latent", "layer"))
    return jax.shard_map(local, mesh=mesh, in_specs=in_specs, out_specs=out_specs, check_vma=False)
```

```python
import functools

import jax
import jax.numpy as jnp
from jax import lax
from jax.experimental import pallas as pl
from jax.experimental.pallas import tpu as pltpu
from jax.sharding import PartitionSpec as P

MESH = pl.DeviceIdType.MESH
F32 = jnp.float32
BF16 = jnp.bfloat16


def exchange_kernel(
    layers, blocks, rscale,
    x_hbm, mlp_hbm, w_hbm, bias_hbm, v_hbm,
    dec_out, xg_out, pg_out,
    xg, mlp, w, bias_all, v, part_send, part_recv, pre, lat, recon, core_send, core_recv, rs_send, rs_recv, og,
    bys, byr, bown, bof, bzs, bzr, bzso, bzro, pg, dec,
    x_ss, x_rs, p_ss, p_rs, z_ss, z_rs, zo_ss, zo_rs, y_ss, y_rs, core_ss, core_rs, rs_ss, rs_rs, og_ss, og_fs, og_rs,
    by_ss, by_rs, bz_ss, bz_rs, bzo_ss, bzo_rs, f_ss, f_rs, in_sem, dec_sem, out_sem,
):
    p = lax.axis_index("layer")
    q = lax.axis_index("latent")
    t = p // 2
    y = p % 2
    o = 1 - y
    rb = x_hbm.shape[0]
    half = w.shape[1] // 2
    partner = (p + 1 - 2 * y, q)
    up = (p + 2, q)
    down = (p - 2, q)
    chips = blocks // 2

    def blk(k):
        return ((q // 2 + k // 2) % chips) * 2 + (q % 2 + k % 2) % 2

    def rows(b):
        return pl.ds(pl.multiple_of(b * rb, rb), rb)

    def cols(h):
        return pl.ds(pl.multiple_of(h * half, half), half)

    def rcopy(src, dst, ss, rs, dev):
        return pltpu.make_async_remote_copy(
            src_ref=src, dst_ref=dst, send_sem=ss, recv_sem=rs, device_id=dev, device_id_type=MESH
        )

    own_x = pltpu.make_async_copy(x_hbm, xg.at[rows(q)], in_sem.at[0])
    w_copy = pltpu.make_async_copy(w_hbm, w, in_sem.at[1])
    bias_copy = pltpu.make_async_copy(bias_hbm, bias_all, in_sem.at[2])
    mlp_copy = pltpu.make_async_copy(mlp_hbm, mlp, in_sem.at[3])
    v_copy = pltpu.make_async_copy(v_hbm, v, in_sem.at[4])
    for copy in (own_x, w_copy, bias_copy, mlp_copy, v_copy):
        copy.start()
    both_up = list(range(blocks - max(blocks // 4, 1), blocks))
    one_up = list(range(blocks - max(blocks // 4, 1)))
    both_down = list(range(blocks - max(blocks // 4, 1), blocks))
    one_down = list(range(blocks - max(blocks // 4, 1)))

    barrier = pltpu.get_barrier_semaphore()
    for k in range(1, blocks):
        pl.semaphore_signal(barrier, inc=1, device_id=(p, blk(k)), device_id_type=MESH)
    pl.semaphore_signal(barrier, inc=1, device_id=partner, device_id_type=MESH)

    @pl.when(t < layers - 1)
    def _():
        pl.semaphore_signal(barrier, inc=1, device_id=up, device_id_type=MESH)

    @pl.when(t > 0)
    def _():
        pl.semaphore_signal(barrier, inc=1, device_id=down, device_id_type=MESH)

    neighbours = blocks + (t < layers - 1).astype(jnp.int32) + (t > 0).astype(jnp.int32)
    pl.semaphore_wait(barrier, neighbours)

    def x_copy(k):
        return rcopy(x_hbm, xg.at[rows(q)], x_ss.at[k], x_rs.at[q], (p, blk(k)))

    for k in list(range(2, blocks)) + [1]:
        x_copy(k).start()

    def part_copy(b):
        return rcopy(part_send.at[rows(b)], part_recv.at[rows(b)], p_ss.at[b], p_rs.at[b], partner)

    def lat_up(l, b):
        piece = lat.at[l, y, rows(b)]
        return rcopy(piece, piece, z_ss.at[l, b], z_rs.at[l, b], up)

    def lat_up_other(l, b):
        piece = lat.at[l, o, rows(b)]
        return rcopy(piece, piece, zo_ss.at[l, b], zo_rs.at[l, b], up)

    def lat_swap(l, b):
        piece = lat.at[l, y, rows(b)]
        return rcopy(piece, piece, y_ss.at[l, b], y_rs.at[l, b], partner)

    def lat_swap_in(l, b):
        piece = lat.at[l, o, rows(b)]
        return rcopy(piece, piece, y_ss.at[l, b], y_rs.at[l, b], partner)

    def own_block(b):
        part_copy(b).wait_recv()
        total = pre[rows(b), :] + part_recv[rows(b), :] + bias
        pre[rows(b), :] = total
        lat[t, y, rows(b), :] = jnp.maximum(total, 0.0).astype(BF16)

        @pl.when(t < layers - 1)
        def _():
            lat_up(t, b).start()

        lat_swap(t, b).start()

    def relay(l, k):
        b = blk(k)
        lat_up(l, b).wait_recv()

        @pl.when(t < layers - 1)
        def _():
            lat_up(l, b).start()

        if k in one_up:
            lat_swap(l, b).start()

    def relay_below(k):
        @pl.when(t > 0)
        def _():
            relay(t - 1, k)

    bias_copy.wait()
    bias_half = jnp.where(y == 0, bias_all[:, :half], bias_all[:, half:])
    own_row = lax.broadcasted_iota(jnp.int32, bias_half.shape, 0) == t
    bias = jnp.sum(jnp.where(own_row, bias_half, 0.0), axis=0, keepdims=True)
    own_x.wait()
    w_copy.wait()
    for k in range(blocks):
        b = blk(k)
        if k > 0:
            rcopy(x_hbm, xg.at[rows(b)], x_ss.at[k], x_rs.at[b], (p, b)).wait_recv()
        part_send[rows(b), :] = jnp.dot(xg[rows(b), :], w[:, cols(o)], preferred_element_type=F32)
        part_copy(b).start()
        pre[rows(b), :] = jnp.dot(xg[rows(b), :], w[:, cols(y)], preferred_element_type=F32)
        if k > 0:
            own_block(blk(k - 1))
        if k > 1:
            relay_below(k - 2)
    own_block(blk(blocks - 1))
    relay_below(blocks - 2)
    relay_below(blocks - 1)
    xg_copy = pltpu.make_async_copy(xg, xg_out, out_sem.at[0])
    xg_copy.start()

    recon[...] = jnp.zeros_like(recon)
    v_copy.wait()

    def decode(l, h):
        recon[...] += jnp.dot(lat[l, h], v[l, cols(h), :], preferred_element_type=F32)

    def other_up(l, b):
        @pl.when(t < layers - 1)
        def _():
            lat_up_other(l, b).start()

    def forward(s, carry):
        l = t - s

        @pl.when(jnp.logical_and(s > 1, s <= t))
        def _():
            for k in range(blocks):
                relay(l, k)

        @pl.when(s <= t)
        def _():
            decode(l, y)

        @pl.when(s > 0)
        def _():
            for k in both_up:
                b = blk(k)

                @pl.when(s == 1)
                def _():
                    lat_swap_in(t, b).wait_recv()

                @pl.when(s > 1)
                def _():
                    lat_up_other(l + 1, b).wait_recv()

                other_up(l + 1, b)
            for k in one_up:
                lat_swap_in(l + 1, blk(k)).wait_recv()
            decode(l + 1, o)

        return carry

    lax.fori_loop(0, t + 2, forward, 0)

    def core_copy(c):
        return rcopy(core_send.at[c], core_recv.at[c], core_ss.at[c], core_rs.at[c], (p, blk(1)))

    def rs_copy(c):
        return rcopy(rs_send.at[c], rs_recv.at[q // 2], rs_ss.at[c], rs_rs.at[q // 2], (p, blk(2 * c)))

    def rs_in(c):
        chip = (q // 2 + c) % chips
        return rcopy(rs_send.at[c], rs_recv.at[chip], rs_ss.at[c], rs_rs.at[chip], (p, blk(2 * c)))

    order = list(range(1, chips)) + [0]
    for c in order:
        core_send[c] = recon[rows(blk(2 * c + 1)), :].astype(BF16)
        core_copy(c).start()
    for c in order:
        core_copy(c).wait_recv()
        total = recon[rows(blk(2 * c)), :] + core_recv[c].astype(F32)
        if c > 0:
            rs_send[c] = total.astype(BF16)
            rs_copy(c).start()
    mlp_copy.wait()
    for c in range(1, chips):
        rs_in(c).wait_recv()
        total = total + rs_recv[(q // 2 + c) % chips].astype(F32)
    og[rows(q), :] = ((total - mlp[...].astype(F32)) * rscale).astype(BF16)

    def og_copy(src, ss, k):
        return rcopy(og.at[rows(src)], og.at[rows(src)], ss.at[k], og_rs.at[src], (p, blk(k)))

    def og_relay(k):
        return rcopy(og.at[rows(blk(k))], og.at[rows(blk(k))], og_fs.at[k], og_rs.at[blk(k)], (p, blk(1)))

    for k in list(range(2, blocks, 2)) + [1]:
        og_copy(q, og_ss, k).start()
    for k in range(2, blocks, 2):
        og_copy(blk(k), og_ss, k).wait_recv()
        og_relay(k).start()
    for k in range(1, blocks, 2):
        og_copy(blk(k), og_ss, k).wait_recv()

    def by_copy(l, b):
        return rcopy(bys.at[l, rows(b)], byr.at[l, rows(b)], by_ss.at[l, b], by_rs.at[l, b], partner)

    def bz_copy(l, b):
        return rcopy(bzs.at[l, rows(b)], bzr.at[l, rows(b)], bz_ss.at[l, b], bz_rs.at[l, b], down)

    def bz_other(l, b):
        return rcopy(bzso.at[l, rows(b)], bzro.at[l, rows(b)], bzo_ss.at[l, b], bzo_rs.at[l, b], down)

    def dec_copy(l):
        return pltpu.make_async_copy(dec.at[l], dec_out.at[l], dec_sem.at[l])

    def back(l, h):
        return lax.dot_general(
            og[...], v[l, cols(h), :], (((1,), (1,)), ((), ())), preferred_element_type=F32
        )

    def add_own(l, b):
        bz_copy(l, b).wait_recv()
        bown[l, rows(b), :] += bzr[l, rows(b), :].astype(F32)

    def add_other(l, b):
        bz_other(l, b).wait_recv()
        bof[l, rows(b), :] += bzro[l, rows(b), :].astype(F32)

    def send_both(l, b):
        bzs[l, rows(b), :] = bown[l, rows(b), :].astype(BF16)
        bz_copy(l, b).start()
        bzso[l, rows(b), :] = bof[l, rows(b), :].astype(BF16)
        bz_other(l, b).start()

    def swap_sum(l, b):
        bys[l, rows(b), :] = bof[l, rows(b), :].astype(BF16)
        by_copy(l, b).start()

    def produce(l, carry):
        bof[l] = back(l, o)

        @pl.when(jnp.logical_and(t == layers - 1, l == t))
        def _():
            for k in both_down:
                swap_sum(l, blk(k))

        for k in one_down:
            swap_sum(l, blk(k))
        bown[l] = back(l, y)

        @pl.when(t == layers - 1)
        def _():
            for k in both_down:
                b = blk(k)

                @pl.when(l < t)
                def _():
                    send_both(l, b)

        return carry

    lax.fori_loop(0, t + 1, produce, 0)

    def collected(l, b):
        by_copy(l, b).wait_recv()
        return bown[l, rows(b), :] + byr[l, rows(b), :].astype(F32)

    def dec_piece(l):
        for h in range(2):
            piece = lax.dot_general(
                lat[l, h], og[...], (((0,), (0,)), ((), ())), preferred_element_type=F32
            )
            dec[l, h * half:(h + 1) * half, :] = piece.astype(BF16)
        dec_copy(l).start()

    def combine_both(l, carry):
        for k in both_down:
            b = blk(k)
            add_own(l, b)
            add_other(l, b)

            @pl.when(l < t)
            def _():
                send_both(l, b)

            @pl.when(l == t)
            def _():
                swap_sum(l, b)

        return carry

    @pl.when(t < layers - 1)
    def _():
        lax.fori_loop(0, t + 1, combine_both, 0)

    def combine(l, carry):
        @pl.when(l < t)
        def _():
            for k in one_down:
                b = blk(k)

                @pl.when(t < layers - 1)
                def _():
                    add_own(l, b)

                bzs[l, rows(b), :] = collected(l, b).astype(BF16)
                bz_copy(l, b).start()

        dec_piece(l)
        return carry

    lax.fori_loop(0, t + 1, combine, 0)

    def blank(l, carry):
        dec[l] = jnp.zeros((2 * half, dec.shape[2]), BF16)
        dec_copy(l).start()
        return carry

    lax.fori_loop(t + 1, layers, blank, 0)

    def final_copy(h, b):
        piece = pg.at[h, rows(b)]
        return rcopy(piece, piece, f_ss.at[b], f_rs.at[b], partner)

    for k in both_down + one_down:
        b = blk(k)
        if k in one_down:
            @pl.when(t < layers - 1)
            def _():
                add_own(t, b)

        value = jnp.where(pre[rows(b), :] > 0.0, collected(t, b), 0.0)
        pg[y, rows(b), :] = value.astype(BF16)
        final_copy(y, b).start()
    for b in range(blocks):
        final_copy(o, b).wait_recv()
    own_dma = pltpu.make_async_copy(pg.at[y], pg_out.at[:, cols(y)], out_sem.at[1])
    other_dma = pltpu.make_async_copy(pg.at[o], pg_out.at[:, cols(o)], out_sem.at[2])
    own_dma.start()
    other_dma.start()

    for k in range(1, blocks):
        x_copy(k).wait_send()
    for c in range(chips):
        core_copy(c).wait_send()
        if c > 0:
            rs_copy(c).wait_send()
    for k in list(range(2, blocks, 2)) + [1]:
        og_copy(q, og_ss, k).wait_send()
    for k in range(2, blocks, 2):
        og_relay(k).wait_send()
    for b in range(blocks):
        part_copy(b).wait_send()
        final_copy(y, b).wait_send()

    def drain(l, carry):
        for k in range(blocks):
            b = blk(k)

            @pl.when(jnp.logical_or(l == t, k in one_up))
            def _():
                lat_swap(l, b).wait_send()

            @pl.when(jnp.logical_or(l == t, k in one_down))
            def _():
                by_copy(l, b).wait_send()

            @pl.when(t < layers - 1)
            def _():
                lat_up(l, b).wait_send()
                if k in both_up:
                    lat_up_other(l, b).wait_send()

            @pl.when(l < t)
            def _():
                bz_copy(l, b).wait_send()
                if k in both_down:
                    bz_other(l, b).wait_send()

        return carry

    lax.fori_loop(0, t + 1, drain, 0)
    for l in range(layers):
        dec_copy(l).wait()
    xg_copy.wait()
    own_dma.wait()
    other_dma.wait()


def exchange(layer_inputs, mlp_outputs, enc_weight, enc_bias, dec_weight):
    layers, latents, width = dec_weight.shape
    blocks = lax.axis_size("latent")
    rb, depth = layer_inputs.shape
    total_rows = rb * blocks
    half = latents // 2
    rscale = total_rows ** (-0.5)
    hbm = pl.BlockSpec(memory_space=pltpu.HBM)
    dma = pltpu.SemaphoreType.DMA
    per_block = dma((blocks,))
    per_layer = dma((layers, blocks))
    sums = pltpu.VMEM((layers, total_rows, half), F32)
    sent = pltpu.VMEM((layers, total_rows, half), BF16)
    one_half = pltpu.VMEM((total_rows, half), F32)
    row_blocks = pltpu.VMEM((blocks // 2, rb, width), BF16)
    per_chip = dma((blocks // 2,))
    return pl.pallas_call(
        functools.partial(exchange_kernel, layers, blocks, rscale),
        out_shape=(
            jax.ShapeDtypeStruct((layers, latents, width), BF16),
            jax.ShapeDtypeStruct((total_rows, depth), BF16),
            jax.ShapeDtypeStruct((total_rows, latents), BF16),
        ),
        in_specs=[hbm] * 5,
        out_specs=(pl.BlockSpec(memory_space=pl.ANY),) * 3,
        scratch_shapes=[
            pltpu.VMEM((total_rows, depth), BF16),
            pltpu.VMEM((rb, width), BF16),
            pltpu.VMEM((depth, latents), BF16),
            pltpu.VMEM((layers, latents), F32),
            pltpu.VMEM((layers, latents, width), BF16),
            one_half, one_half, one_half,
            pltpu.VMEM((layers, 2, total_rows, half), BF16),
            pltpu.VMEM((total_rows, width), F32),
            row_blocks, row_blocks, row_blocks, row_blocks,
            pltpu.VMEM((total_rows, width), BF16),
            sent, sent, sums, sums, sent, sent, sent, sent,
            pltpu.VMEM((2, total_rows, half), BF16),
            pltpu.VMEM((layers, latents, width), BF16),
            per_block, per_block, per_block, per_block,
            per_layer, per_layer, per_layer, per_layer, per_layer, per_layer,
            per_chip, per_chip, per_chip, per_chip, per_block, per_block, per_block,
            per_layer, per_layer, per_layer, per_layer, per_layer, per_layer,
            per_block, per_block,
            dma((5,)), dma((layers,)), dma((3,)),
        ],
        compiler_params=pltpu.CompilerParams(
            collective_id=0, has_side_effects=True, vmem_limit_bytes=56 * 2**20
        ),
        name="exchange",
    )(layer_inputs, mlp_outputs, enc_weight, enc_bias, dec_weight)


def finish_kernel(
    xg_hbm, pg_hbm, dec_hbm, enc_out, dec_out, xg, pg, enc, dec, in_sem, dec_in, dec_sem, enc_sem
):
    layers = dec.shape[0]
    piece = enc.shape[0] // layers
    ins = [
        pltpu.make_async_copy(xg_hbm, xg, in_sem.at[0]),
        pltpu.make_async_copy(pg_hbm, pg, in_sem.at[1]),
    ]
    reads = [pltpu.make_async_copy(dec_hbm.at[l], dec.at[l], dec_in.at[l]) for l in range(layers)]
    for copy in ins + reads:
        copy.start()
    for copy in ins:
        copy.wait()
    writes = []
    for l in range(layers):
        part = pl.ds(l * piece, piece)
        enc[part, :] = lax.dot_general(
            xg[:, part], pg[...], (((0,), (0,)), ((), ())), preferred_element_type=F32
        )
        writes.append(pltpu.make_async_copy(enc.at[part], enc_out.at[part], enc_sem.at[l]))
        writes[-1].start()
        reads[l].wait()
        writes.append(pltpu.make_async_copy(dec.at[l], dec_out.at[l], dec_sem.at[l]))
        writes[-1].start()
    for copy in writes:
        copy.wait()


def local(layer_inputs, mlp_outputs, enc_weight, enc_bias, dec_weight):
    dec, xg, pg = exchange(layer_inputs, mlp_outputs, enc_weight, enc_bias, dec_weight)
    hbm = pl.BlockSpec(memory_space=pltpu.HBM)
    per_layer = pltpu.SemaphoreType.DMA((dec.shape[0],))
    return pl.pallas_call(
        finish_kernel,
        in_specs=[hbm] * 3,
        out_specs=(hbm,) * 2,
        out_shape=(
            jax.ShapeDtypeStruct(enc_weight.shape, F32),
            jax.ShapeDtypeStruct(dec_weight.shape, BF16),
        ),
        scratch_shapes=[
            pltpu.VMEM(xg.shape, BF16),
            pltpu.VMEM(pg.shape, BF16),
            pltpu.VMEM(enc_weight.shape, F32),
            pltpu.VMEM(dec.shape, BF16),
            pltpu.SemaphoreType.DMA((2,)),
            per_layer, per_layer, per_layer,
        ],
        compiler_params=pltpu.CompilerParams(vmem_limit_bytes=56 * 2**20),
        name="finish",
    )(xg, pg, dec)


def solution(mesh):
    in_specs = (
        P("latent", "layer"),
        P("latent", "layer"),
        P("layer", "latent"),
        P(None, "latent"),
        P(None, "latent", "layer"),
    )
    out_specs = (P("layer", "latent"), P(None, "latent", "layer"))
    return jax.shard_map(local, mesh=mesh, in_specs=in_specs, out_specs=out_specs, check_vma=False)
```
